32 devices in a mesh: dp: 8 (over z, x), tok: 4 (over y, core).
Axes of the slice: x: 2, y: 2, z: 4, core: 2. Of those that a mesh axis runs over, the one named last changes fastest.
Arguments:
- inputs: bfloat16 [128, 200, 384], P(('dp', 'tok')), may hold values from -6 to 6
- cotangent: bfloat16 [128, 200, 384], P(('dp', 'tok')), may hold values from -6 to 6
- lengths: int32 [128], P('dp'), may hold values from 1 to 198, 12672 in all
- w_qkv: float32 [2, 384, 1152], P(None, None, 'dp'), may hold values from -0.3125 to 0.3125
- w_proj: float32 [2, 384, 384], P(None, None, 'dp'), may hold values from -0.875 to 0.875
- w_fc1: float32 [2, 384, 1536], P(None, None, 'dp'), may hold values from -0.3125 to 0.3125
- w_fc2: float32 [2, 1536, 384], P(None, 'dp'), may hold values from -0.15625 to 0.15625
- norm_gains: float32 [2, 2, 384], P(None, None, 'dp'), may hold values from 0.5 to 1.5
- biases: float32 [2, 3840], P(None, 'dp'), may hold values from -1.75 to 1.75
- mom_qkv: float32 [2, 2, 384, 1152], P(None, None, None, 'dp'), as said below
- mom_proj: float32 [2, 2, 384, 384], P(None, None, None, 'dp'), as said below
- mom_fc1: float32 [2, 2, 384, 1536], P(None, None, None, 'dp'), as said below
- mom_fc2: float32 [2, 2, 1536, 384], P(None, None, 'dp'), as said below
- mom_gains: float32 [2, 2, 2, 384], P(None, None, None, 'dp'), as said below
- mom_biases: float32 [2, 2, 3840], P(None, None, 'dp'), as said below
Outputs:
- layer_out: bfloat16 [128, 200, 384], P(('dp', 'tok'))
- input_grad: float32 [128, 200, 384], P(('dp', 'tok'))
- grad_norm: float32 [], replicated
- state_qkv: float32 [2, 2, 384, 1152], P(None, None, None, 'dp')
- state_proj: float32 [2, 2, 384, 384], P(None, None, None, 'dp')
- state_fc1: float32 [2, 2, 384, 1536], P(None, None, None, 'dp')
- state_fc2: float32 [2, 2, 1536, 384], P(None, None, 'dp')
- state_gains: float32 [2, 2, 2, 384], P(None, None, None, 'dp')
- state_biases: float32 [2, 2, 3840], P(None, None, 'dp')
- second_moments: float32 [3548160], P('dp')
The draws below stay inside these ranges and needn't reach their ends.
Inputs may be any that keep to these rules, and one draw needn't show every extreme that they name: Sequence i keeps its first lengths[i] slots; some sequence keeps all 198. `mom_qkv`: index 0 holds the first moment, index 1 the second moment, which is positive. `mom_proj`: index 0 holds the first moment, index 1 the second moment, which is positive. `mom_fc1`: index 0 holds the first moment, index 1 the second moment, which is positive. `mom_fc2`: index 0 holds the first moment, index 1 the second moment, which is positive. `mom_gains`: index 0 holds the first moment, index 1 the second moment, which is positive. `mom_biases`: index 0 holds the first moment, index 1 the second moment, which is positive.
All inputs are finite; a program needn't handle non-finite values. No bound on the sum of `lengths` on one device may be relied on, other than what follows from the above.
Results may differ from the reference program's by a relative error of at most 0.018.
The reference program's roundings to bfloat16 on the way count: a program that leaves them out, or rounds other values in their place, can miss the bound.
Values may be sent and summed in bfloat16 or wider, within the bound.
No kernel may reach another device: no remote copies, remote signals or barrier semaphores. Data moves between devices by JAX's collectives and lax.ppermute only.
A program may use at most 128 MiB of HBM per device.

```python
import math
import jax
import jax.numpy as jnp
import numpy as np
from jax import lax

D = 384
HEADS = 6
HD = 64
FF = 1536
LEN = 198
SLOTS = 200
LAYERS = 2
STEP = 10
SEQS = 128
N_DP = 8


def moment_pair(key, dims_of, scale):
    first_mom = jax.random.normal(jax.random.fold_in(key, 1), dims_of, jnp.float32) * (0.111 * scale)
    spread = jax.random.uniform(jax.random.fold_in(key, 2), dims_of, jnp.float32, -0.6931, 2.0794)
    second_mom = jnp.exp(spread) * (0.001 * scale * scale)
    return jnp.stack([first_mom, second_mom])


def draw_mom_qkv(key, part):
    return moment_pair(jax.random.fold_in(key, 11), (LAYERS, D, 3 * D), 0.25)


def draw_mom_proj(key, part):
    return moment_pair(jax.random.fold_in(key, 12), (LAYERS, D, D), 0.25)


def draw_mom_fc1(key, part):
    return moment_pair(jax.random.fold_in(key, 13), (LAYERS, D, FF), 0.25)


def draw_mom_fc2(key, part):
    return moment_pair(jax.random.fold_in(key, 14), (LAYERS, FF, D), 0.25)


def draw_mom_gains(key, part):
    return moment_pair(jax.random.fold_in(key, 15), (LAYERS, 2, D), 0.5)


def draw_mom_biases(key, part):
    return moment_pair(jax.random.fold_in(key, 16), (LAYERS, 6 * D + FF), 0.5)


def levels(key, extent, pieces, smallest, high):
    def one(dim, parts):
        draws = jax.random.uniform(jax.random.fold_in(jax.random.fold_in(key, 6), dim), (parts,), jnp.float32, smallest / len(pieces), high / len(pieces))
        return jnp.repeat(jnp.exp(draws), extent[dim] // parts).reshape((-1,) + (1,) * (len(extent) - dim - 1))

    gain = one(*pieces[0])
    for cut in pieces[1:]:
        gain = gain * one(*cut)
    return gain


def split_up(amount, total, bound, lean):
    weights = [(1 << 20) // math.isqrt(grade ** lean) + 1 for grade in range(2, amount + 1)]
    spare, given = total - bound - (amount - 1), [1] * (amount - 1)
    while spare > 0:
        free = [i for i in range(amount - 1) if given[i] < bound]
        whole, remaining = sum([weights[i] for i in free]), spare
        for i in free:
            extra = min(bound - given[i], max(1, remaining * weights[i] // whole), spare)
            given[i] = given[i] + extra
            spare = spare - extra
    return np.array([bound] + given)


def ragged(stream_key, number_of, total, most, skew):
    if number_of == 2:
        one = jax.random.randint(stream_key, (), max(1, total - most), min(most, total - 1) + 1)
        return jnp.stack([one, total - one])
    sizes = jnp.asarray(split_up(number_of, total, most, skew), jnp.int32)
    pairs = (number_of - 1) // 2
    giver, taker = sizes[1:1 + 2 * pairs:2], sizes[2:2 + 2 * pairs:2]
    margin = jnp.minimum(giver - 1, most - taker)
    moved = jax.random.randint(jax.random.fold_in(stream_key, 1), (pairs,), 0, 1 << 20) % (margin + 1)
    sizes = sizes.at[1:1 + 2 * pairs:2].set(giver - moved).at[2:2 + 2 * pairs:2].set(taker + moved)
    return sizes[jax.random.permutation(jax.random.fold_in(stream_key, 2), number_of)]


def scatter_about(own_key, extent, scale, most, cuts=(), held_as=jnp.bfloat16):
    array = jax.random.normal(own_key, extent, jnp.float32) * scale
    if len(cuts) > 0:
        array = levels(own_key, extent, cuts, -0.22, 0.18) * array
    return jnp.clip(array, min=-most, max=most).astype(held_as)


def setup_inputs(seed: int = 0) -> dict:
    key_of = jax.random.split(jax.random.key(seed), 16)
    inputs = scatter_about(key_of[0], (SEQS, SLOTS, D), 1.0, 6.0, ((0, 32),))
    cotangent = scatter_about(key_of[1], (SEQS, SLOTS, D), 1.0, 6.0, ((0, 32),))
    lengths = ragged(key_of[2], SEQS, SEQS * LEN // 2, LEN, 1).astype(jnp.int32)
    w_qkv = scatter_about(key_of[3], (LAYERS, D, 3 * D), D ** -0.5, 0.3125, ((2, 8),), jnp.float32)
    w_proj = scatter_about(key_of[4], (LAYERS, D, D), (D // 8) ** -0.5, 0.875, ((2, 8),), jnp.float32)
    w_fc1 = scatter_about(key_of[5], (LAYERS, D, FF), D ** -0.5, 0.3125, ((2, 8),), jnp.float32)
    w_fc2 = scatter_about(key_of[6], (LAYERS, FF, D), FF ** -0.5, 0.15625, ((1, 8),), jnp.float32)
    norm_gains = jnp.clip(1.0 + 0.1 * jax.random.normal(key_of[7], (LAYERS, 2, D), jnp.float32), 0.5, 1.5)
    biases = scatter_about(key_of[8], (LAYERS, 6 * D + FF), 0.3, 1.75, ((1, 8),), jnp.float32)
    mom_qkv = draw_mom_qkv(jax.random.fold_in(key_of[15], 71), 0)
    mom_proj = draw_mom_proj(jax.random.fold_in(key_of[15], 71), 0)
    mom_fc1 = draw_mom_fc1(jax.random.fold_in(key_of[15], 71), 0)
    mom_fc2 = draw_mom_fc2(jax.random.fold_in(key_of[15], 71), 0)
    mom_gains = draw_mom_gains(jax.random.fold_in(key_of[15], 71), 0)
    mom_biases = draw_mom_biases(jax.random.fold_in(key_of[15], 71), 0)
    return dict(inputs=inputs, cotangent=cotangent, lengths=lengths, w_qkv=w_qkv, w_proj=w_proj, w_fc1=w_fc1, w_fc2=w_fc2, norm_gains=norm_gains, biases=biases, mom_qkv=mom_qkv, mom_proj=mom_proj, mom_fc1=mom_fc1, mom_fc2=mom_fc2, mom_gains=mom_gains, mom_biases=mom_biases)


@jax.custom_vjp
def low(v):
    return lax.optimization_barrier(v.astype(jnp.bfloat16)).astype(jnp.float32)

@jax.custom_vjp
def low_back(v):
    return v

def low_keep(v):
    return (low(v), None)

def low_pass(kept, grad):
    return (grad,)

def back_keep(v):
    return (v, None)

def back_low(kept, grad):
    return (low(grad),)
low.defvjp(low_keep, low_pass)
low_back.defvjp(back_keep, back_low)

def layer_norm(hidden, gain_row, shift_row):
    row_mean = lax.optimization_barrier(jnp.mean(hidden, -1, keepdims=True))
    centered = hidden - row_mean
    variance = lax.optimization_barrier(jnp.mean(centered * centered, -1, keepdims=True))
    return centered * lax.rsqrt(variance + 1e-06) * gain_row + shift_row

def attend_block(packed):
    stacked, lens_block = packed
    slot_total = stacked.shape[1]
    query_b = stacked[:, :, 0]
    key_b = stacked[:, :, 1]
    value_b = stacked[:, :, 2]
    scores = jnp.einsum('bqhd,bkhd->bhqk', query_b, key_b, precision=lax.Precision.HIGHEST) * 0.125
    scores = low_back(scores)
    key_mask = jnp.arange(slot_total).astype(jnp.int32)[None, :] < lens_block[:, None]
    scores = jnp.where(key_mask[:, None, None, :], scores, -1e+30)
    prob_low = low(jax.nn.softmax(scores, axis=-1))
    return jnp.einsum('bhqk,bkhd->bqhd', prob_low, value_b, precision=lax.Precision.HIGHEST)

def forward(params, hidden, lengths):
    w_qkv, w_proj, w_fc1, w_fc2, norm_gains, biases = params
    seq_total = lengths.shape[0]
    row_total = hidden.shape[0]
    slot_total = row_total // seq_total
    block_count = seq_total // 8
    lens_blocks = lengths.reshape(block_count, 8)
    highest = lax.Precision.HIGHEST
    for layer_id in range(LAYERS):
        q_weight = low(w_qkv[layer_id])
        o_weight = low(w_proj[layer_id])
        up_weight = low(w_fc1[layer_id])
        down_weight = low(w_fc2[layer_id])
        gain_rows = low(norm_gains[layer_id])
        bias_row = low(biases[layer_id])
        a_first = low(layer_norm(hidden, gain_rows[0], bias_row[0:D]))
        qkv_bias = jnp.concatenate([bias_row[D:2 * D], jnp.zeros((D,), jnp.float32), bias_row[2 * D:3 * D]])
        qkv = jnp.dot(a_first, q_weight, precision=highest) + qkv_bias
        qkv = low(low_back(qkv)).reshape(block_count, 8, slot_total, 3, HEADS, HD)
        attended = lax.map(jax.checkpoint(attend_block), (qkv, lens_blocks))
        attended = low(low_back(attended.reshape(row_total, D)))
        hidden = hidden + low_back(jnp.dot(attended, o_weight, precision=highest) + bias_row[3 * D:4 * D])
        a_second = low(layer_norm(hidden, gain_rows[1], bias_row[4 * D:5 * D]))
        pre_act = low_back(jnp.dot(a_second, up_weight, precision=highest) + bias_row[6 * D:])
        activated = low(jax.nn.gelu(pre_act, approximate=False))
        hidden = hidden + low_back(jnp.dot(activated, down_weight, precision=highest) + bias_row[5 * D:6 * D])
    valid = (jnp.arange(slot_total).astype(jnp.int32)[None, :] < lengths[:, None]).reshape(row_total, 1)
    return jnp.where(valid, hidden, 0.0)

def adamw(weight, moments, clipped, rate, decay):
    first_mom = 0.9 * moments[0] + 0.1 * clipped
    second_mom = 0.999 * moments[1] + 0.001 * clipped * clipped
    fixed_first = first_mom / (1.0 - 0.9 ** STEP)
    fixed_second = second_mom / (1.0 - 0.999 ** STEP)
    new_weight = weight - rate * (fixed_first / (jnp.sqrt(fixed_second) + 1e-08) + decay * weight)
    return (jnp.stack([new_weight, first_mom]), second_mom)

def owner_blocks(tensor, split_dim):
    old_shape = tensor.shape
    new_shape = old_shape[:split_dim] + (N_DP, old_shape[split_dim] // N_DP) + old_shape[split_dim + 1:]
    moved_axes = jnp.moveaxis(tensor.reshape(new_shape), split_dim, 0)
    return moved_axes.reshape(N_DP, -1)

def reference(inputs, cotangent, lengths, w_qkv, w_proj, w_fc1, w_fc2, norm_gains, biases, mom_qkv, mom_proj, mom_fc1, mom_fc2, mom_gains, mom_biases):
    row_total = inputs.shape[0] * inputs.shape[1]
    params = (w_qkv, w_proj, w_fc1, w_fc2, norm_gains, biases)

    def apply_net(weights, acts):
        return forward(weights, acts, lengths)
    outputs, pullback = jax.vjp(apply_net, params, inputs.astype(jnp.float32).reshape(row_total, D))
    grads, grad_in = pullback(cotangent.astype(jnp.float32).reshape(row_total, D))
    squares = jnp.sum(grads[0] * grads[0]) + jnp.sum(grads[1] * grads[1]) + jnp.sum(grads[2] * grads[2])
    squares = squares + jnp.sum(grads[3] * grads[3]) + jnp.sum(grads[4] * grads[4]) + jnp.sum(grads[5] * grads[5])
    grad_norm = jnp.sqrt(squares)
    limit = 0.25 * math.sqrt(LAYERS * (4 * D * D + 2 * D * FF + 8 * D + FF))
    factor = jnp.minimum(1.0, limit / (grad_norm + 1e-06))
    state_qkv, second_qkv = adamw(w_qkv, mom_qkv, grads[0] * factor, 0.08, 0.05)
    state_proj, second_proj = adamw(w_proj, mom_proj, grads[1] * factor, 0.08, 0.05)
    state_fc1, second_fc1 = adamw(w_fc1, mom_fc1, grads[2] * factor, 0.08, 0.05)
    state_fc2, second_fc2 = adamw(w_fc2, mom_fc2, grads[3] * factor, 0.08, 0.05)
    state_gains, second_gains = adamw(norm_gains, mom_gains, grads[4] * factor, 0.4, 0.0)
    state_biases, second_biases = adamw(biases, mom_biases, grads[5] * factor, 0.4, 0.0)
    second_moments = jnp.concatenate([owner_blocks(second_qkv, 2), owner_blocks(second_proj, 2), owner_blocks(second_fc1, 2), owner_blocks(second_fc2, 1), owner_blocks(second_gains, 2), owner_blocks(second_biases, 1)], 1).reshape(-1)
    layer_out = outputs.astype(jnp.bfloat16).reshape(inputs.shape)
    input_grad = grad_in.reshape(inputs.shape)
    return (layer_out, input_grad, grad_norm, state_qkv, state_proj, state_fc1, state_fc2, state_gains, state_biases, second_moments)
```

```python
import functools
import math

import jax
import jax.numpy as jnp
from jax import lax
from jax.experimental import pallas as pl
from jax.experimental.pallas import tpu as pltpu
from jax.sharding import PartitionSpec as P

D = 384
HEADS = 6
HD = 64
FF = 1536
LAYERS = 2
STEP = 10
PAIRS = HEADS // 2
TILE = 128
EPS = 1e-06
HALF_ROOT = 0.7071067811865476
INV_ROOT_TAU = 0.3989422804014327
LOG2E = 1.4426950408889634
SCORE = 0.125 * LOG2E
TAIL_P = 0.4
TAIL = (
    0.22480539044849576,
    0.2382192213985389,
    0.13072083829499273,
    0.43284363894582684,
    -0.41172890451981375,
    0.7191256145749827,
    -0.41194367033429247,
    0.07795786677173361,
)
BF = jnp.bfloat16
F32 = jnp.float32


def nn(a, b):
    return lax.dot_general(a, b, (((1,), (0,)), ((), ())), preferred_element_type=F32)


def nt(a, b):
    return lax.dot_general(a, b, (((1,), (1,)), ((), ())), preferred_element_type=F32)


def tn(a, b):
    return lax.dot_general(a, b, (((0,), (0,)), ((), ())), preferred_element_type=F32)


def normalize(hidden):
    centered = hidden - jnp.mean(hidden, -1, keepdims=True)
    variance = jnp.mean(centered * centered, -1, keepdims=True)
    inverse = lax.rsqrt(variance + EPS)
    return centered * inverse, inverse


def norm_back(grad_n, normed, inverse):
    first = jnp.mean(grad_n, -1, keepdims=True)
    second = jnp.mean(grad_n * normed, -1, keepdims=True)
    return inverse * (grad_n - first - normed * second)


def gelu_pair(u):
    t = 1.0 / (1.0 + (TAIL_P * HALF_ROOT) * jnp.abs(u))
    bell = jnp.exp2(u * u * (-0.5 * LOG2E))
    poly = jnp.full_like(t, 0.5 * TAIL[-1])
    for coef in TAIL[-2::-1]:
        poly = poly * t + 0.5 * coef
    low = poly * t * bell
    cdf = jnp.where(u < 0.0, low, 1.0 - low)
    return u * cdf, cdf + u * bell * INV_ROOT_TAU


def rows_of(t):
    return pl.ds(pl.multiple_of(t * TILE, TILE), TILE)


def zero_tail(tiles, total, refs):
    def body(t, carry):
        for ref in refs:
            ref[rows_of(t), :] = jnp.zeros((TILE, ref.shape[1]), ref.dtype)
        return carry

    lax.fori_loop(tiles, total, body, 0)


def phase_qkv(tiles, h_ref, vec_ref, qkv_w, a_ref, qkv_ref):
    def body(t, carry):
        rows = rows_of(t)
        normed, _ = normalize(h_ref[rows, :])
        a = (normed * vec_ref[0:1, 0:D] + vec_ref[1:2, 0:D]).astype(BF)
        a_ref[rows, :] = a
        qkv_ref[rows, :] = (nt(a, qkv_w[...]) + vec_ref[7:8, 0 : 3 * D]).astype(BF)
        return carry

    lax.fori_loop(0, tiles, body, 0)


def head_mask(x, side):
    lane = lax.broadcasted_iota(jnp.int32, x.shape, 1)
    keep = (lane < HD) if side == 0 else (lane >= HD)
    return jnp.where(keep, x, jnp.zeros_like(x))


def pick(a, b):
    lane = lax.broadcasted_iota(jnp.int32, a.shape, 1)
    return jnp.where(lane < HD, a, b)


def attend(meta, seqs, slots, qkv_ref, o_ref, lse_ref):
    widths = window_sizes(slots)

    def seq_body(i, carry):
        length, start = meta[i], pl.multiple_of(meta[seqs + i], 16)

        def run(width):
            rows = pl.ds(start, width)
            for pair in range(PAIRS):
                at = pair * 2 * HD
                q = qkv_ref[rows, at : at + 2 * HD]
                k = qkv_ref[rows, D + at : D + at + 2 * HD]
                v = qkv_ref[rows, 2 * D + at : 2 * D + at + 2 * HD]
                outs = []
                for side in range(2):
                    s = nt(head_mask(k, side), q)
                    keep = lax.broadcasted_iota(jnp.int32, s.shape, 0) < length
                    s = jnp.where(keep, s, -1e30)
                    top = jnp.max(s, 0, keepdims=True)
                    e = jnp.exp2((s - top) * SCORE)
                    total = jnp.sum(e, 0, keepdims=True)
                    p = (e * (1.0 / total)).astype(BF)
                    outs.append(tn(p, v))
                    row = pair * 2 + side
                    lse_ref[i, row : row + 1, 0:width] = top * SCORE + jnp.log2(total)
                o_ref[rows, at : at + 2 * HD] = pick(*outs).astype(BF)

        low = 0
        for width in widths:
            pl.when(jnp.logical_and(length > low, length <= width))(functools.partial(run, width))
            low = width
        return carry

    lax.fori_loop(0, seqs, seq_body, 0)


def attend_back(meta, seqs, slots, qkv_ref, do_ref, lse_ref, dqkv_ref):
    widths = window_sizes(slots)

    def seq_body(i, carry):
        length, start = meta[i], pl.multiple_of(meta[seqs + i], 16)

        def run(width):
            rows = pl.ds(start, width)
            keep_rows = lax.broadcasted_iota(jnp.int32, (width, 2 * HD), 0) < length
            for pair in range(PAIRS):
                at = pair * 2 * HD
                q = qkv_ref[rows, at : at + 2 * HD]
                k = qkv_ref[rows, D + at : D + at + 2 * HD]
                v = qkv_ref[rows, 2 * D + at : 2 * D + at + 2 * HD]
                do = do_ref[rows, at : at + 2 * HD]
                do = jnp.where(keep_rows, do, jnp.zeros_like(do))
                dqs, dks, dvs = [], [], []
                for side in range(2):
                    s = nt(head_mask(k, side), q)
                    keep = lax.broadcasted_iota(jnp.int32, s.shape, 0) < length
                    row = pair * 2 + side
                    lse = lse_ref[i, row : row + 1, 0:width]
                    p = jnp.where(keep, jnp.exp2(s * SCORE - lse), 0.0)
                    dp = nt(head_mask(v, side), do)
                    inner = jnp.sum(p * dp, 0, keepdims=True)
                    ds = (p * (dp - inner)).astype(BF)
                    dvs.append(nn(p.astype(BF), do))
                    dks.append(nn(ds, q))
                    dqs.append(tn(ds, k))
                dqkv_ref[rows, at : at + 2 * HD] = (pick(*dqs) * 0.125).astype(BF)
                dqkv_ref[rows, D + at : D + at + 2 * HD] = (pick(*dks) * 0.125).astype(BF)
                dqkv_ref[rows, 2 * D + at : 2 * D + at + 2 * HD] = pick(*dvs).astype(BF)

        low = 0
        for width in widths:
            pl.when(jnp.logical_and(length > low, length <= width))(functools.partial(run, width))
            low = width
        return carry

    lax.fori_loop(0, seqs, seq_body, 0)


def window_sizes(slots):
    full = -(-slots // 16) * 16
    return [128, full] if full > 128 else [full]


def phase_mlp(tiles, h_ref, o_ref, vec_ref, proj_w, fc1_w, fc2_w, mid_ref, a_ref, act_ref, slope_ref, out_ref):
    def body(t, carry):
        rows = rows_of(t)
        mid = h_ref[rows, :] + nt(o_ref[rows, :], proj_w[...]) + vec_ref[4:5, 0:D]
        mid_ref[rows, :] = mid
        normed, _ = normalize(mid)
        a = (normed * vec_ref[2:3, 0:D] + vec_ref[3:4, 0:D]).astype(BF)
        a_ref[rows, :] = a
        for c in range(0, FF, 512):
            u = nt(a, fc1_w[c : c + 512, :]) + vec_ref[6:7, c : c + 512]
            act, slope = gelu_pair(u)
            act_ref[rows, c : c + 512] = act.astype(BF)
            slope_ref[rows, c : c + 512] = slope
        out_ref[rows, :] = mid + nn(act_ref[rows, :], fc2_w[...]) + vec_ref[5:6, 0:D]
        return carry

    lax.fori_loop(0, tiles, body, 0)


def add_row(ref, row, width, value):
    ref[row : row + 1, 0:width] += jnp.sum(value, 0, keepdims=True)


def phase_mlp_back(tiles, g_ref, mid_ref, slope_ref, vec_ref, fc1_w, fc2_w, proj_w, dm_ref, du_ref, g1_ref, dp_ref, do_ref, small_ref):
    def body(t, carry):
        rows = rows_of(t)
        g = g_ref[rows, :]
        dm = g.astype(BF)
        dm_ref[rows, :] = dm
        add_row(small_ref, 5, D, dm.astype(F32))
        for c in range(0, FF, 512):
            dact = nt(dm, fc2_w[c : c + 512, :])
            du = (dact * slope_ref[rows, c : c + 512]).astype(BF)
            du_ref[rows, c : c + 512] = du
            small_ref[6:7, c : c + 512] += jnp.sum(du.astype(F32), 0, keepdims=True)
        da = nn(du_ref[rows, :], fc1_w[...])
        normed, inverse = normalize(mid_ref[rows, :])
        add_row(small_ref, 2, D, da * normed)
        add_row(small_ref, 3, D, da)
        g1 = g + norm_back(da * vec_ref[2:3, 0:D], normed, inverse)
        g1_ref[rows, :] = g1
        dp = g1.astype(BF)
        dp_ref[rows, :] = dp
        add_row(small_ref, 4, D, dp.astype(F32))
        do_ref[rows, :] = nn(dp, proj_w[...]).astype(BF)
        return carry

    lax.fori_loop(0, tiles, body, 0)


def phase_qkv_back(tiles, h_ref, g1_ref, dqkv_ref, vec_ref, qkv_w, g_out, small_ref):
    def body(t, carry):
        rows = rows_of(t)
        dqkv = dqkv_ref[rows, :]
        add_row(small_ref, 7, 3 * D, dqkv.astype(F32))
        da = nn(dqkv, qkv_w[...])
        normed, inverse = normalize(h_ref[rows, :])
        add_row(small_ref, 0, D, da * normed)
        add_row(small_ref, 1, D, da)
        g_out[rows, :] = g1_ref[rows, :] + norm_back(da * vec_ref[0:1, 0:D], normed, inverse)
        return carry

    lax.fori_loop(0, tiles, body, 0)


def outer_products(tiles, total, jobs):
    half = -(-total // 2) * TILE
    rows = total * TILE
    step = 128
    for left, right, store in jobs:
        def body(m, carry, left=left, right=right, store=store):
            cols = pl.ds(pl.multiple_of(m * step, step), step)
            first = lambda: tn(left[0:half, cols], right[0:half, :])
            both = lambda: tn(left[0:rows, cols], right[0:rows, :])
            store(m * step, lax.cond(tiles * TILE > half, both, first))
            return carry

        lax.fori_loop(0, left.shape[1] // step, body, 0)


def store_rows(ref, base):
    def store(first, block):
        ref[pl.ds(pl.multiple_of(base + first, 128), 128), :] = block.astype(ref.dtype)

    return store


def vmem(n):
    return [pl.BlockSpec(memory_space=pltpu.VMEM)] * n


def call(body, name, outs, scratch, meta, *arrays):
    shapes = [jax.ShapeDtypeStruct(s, d) for s, d in outs]
    return pl.pallas_call(
        body,
        name=name,
        out_shape=shapes,
        in_specs=[pl.BlockSpec(memory_space=pltpu.SMEM)] + vmem(len(arrays)),
        out_specs=vmem(len(outs)),
        scratch_shapes=[pltpu.VMEM(s, d) for s, d in scratch],
        compiler_params=pltpu.CompilerParams(vmem_limit_bytes=56 << 20),
    )(meta, *arrays)


def plan_rows(lengths, slots):
    seqs = lengths.shape[0]
    room = (lengths + 15) // 16 * 16
    ends = jnp.cumsum(room)
    tiles = (ends[-1:] + TILE - 1) // TILE
    return jnp.concatenate([lengths, ends - room, tiles]).astype(jnp.int32)


def packed_tiles(seqs, slots):
    full = -(-slots // 16) * 16
    return -(-(seqs * full) // TILE)


def first_half(seqs, slots, total):
    rows = total * TILE

    def body(meta, x_ref, vec, qkv_w, h_ref, a_ref, qkv_ref, o_ref, lse_ref):
        tiles = meta[2 * seqs]
        h_ref[...] = jnp.zeros_like(h_ref)
        for i in range(seqs):
            at = pl.multiple_of(meta[seqs + i], 16)
            h_ref[pl.ds(at, slots), :] = x_ref[i].astype(F32)
        phase_qkv(tiles, h_ref, vec, qkv_w, a_ref, qkv_ref)
        zero_tail(tiles, total, [a_ref, qkv_ref])
        o_ref[...] = jnp.zeros_like(o_ref)
        attend(meta, seqs, slots, qkv_ref, o_ref, lse_ref)

    def run(meta, x, vec, qkv_w):
        outs = [((rows, D), F32), ((rows, D), BF), ((rows, 3 * D), BF), ((rows, D), BF), ((seqs, 8, 256), F32)]
        return call(body, "first_half", outs, [], meta, x, vec, qkv_w)

    return run


def middle(seqs, slots, total):
    rows = total * TILE

    def body(meta, h0, o0, vec0, proj_w, fc1_w, fc2_w, vec1, qkv_w, mid, a2, act, slope, h1, a1, qkv, o, lse):
        tiles = meta[2 * seqs]
        phase_mlp(tiles, h0, o0, vec0, proj_w, fc1_w, fc2_w, mid, a2, act, slope, h1)
        zero_tail(tiles, total, [a2, act])
        phase_qkv(tiles, h1, vec1, qkv_w, a1, qkv)
        zero_tail(tiles, total, [a1, qkv])
        o[...] = jnp.zeros_like(o)
        attend(meta, seqs, slots, qkv, o, lse)

    def run(meta, *args):
        outs = [
            ((rows, D), F32), ((rows, D), BF), ((rows, FF), BF), ((rows, FF), F32), ((rows, D), F32),
            ((rows, D), BF), ((rows, 3 * D), BF), ((rows, D), BF), ((seqs, 8, 256), F32),
        ]
        return call(body, "middle", outs, [], meta, *args)

    return run


def turn(seqs, slots, total):
    rows = total * TILE

    def body(meta, h, o, vec, proj_w, fc1_w, fc2_w, cot, out_ref, grads, small, g1, dp, do, mid, a2, act, slope, h2, dm, du):
        tiles = meta[2 * seqs]
        phase_mlp(tiles, h, o, vec, proj_w, fc1_w, fc2_w, mid, a2, act, slope, h2)
        for i in range(seqs):
            at = pl.multiple_of(meta[seqs + i], 16)
            keep = lax.broadcasted_iota(jnp.int32, (slots, D), 0) < meta[i]
            out_ref[i] = jnp.where(keep, h2[pl.ds(at, slots), :], 0.0).astype(out_ref.dtype)
        h2[...] = jnp.zeros_like(h2)
        for i in range(seqs):
            at = pl.multiple_of(meta[seqs + i], 16)
            keep = lax.broadcasted_iota(jnp.int32, (slots, D), 0) < meta[i]
            h2[pl.ds(at, slots), :] = jnp.where(keep, cot[i].astype(F32), 0.0)
        small[...] = jnp.zeros_like(small)
        phase_mlp_back(tiles, h2, mid, slope, vec, fc1_w, fc2_w, proj_w, dm, du, g1, dp, do, small)
        zero_tail(tiles, total, [a2, act, dm, du, dp, do])
        outer_products(tiles, total, [(du, a2, store_rows(grads, 0)), (act, dm, store_rows(grads, FF))])

    def run(meta, h, o, vec, proj_w, fc1_w, fc2_w, cot):
        outs = [
            (cot.shape, BF), ((2 * FF, D), BF), ((8, FF), F32), ((rows, D), F32), ((rows, D), BF), ((rows, D), BF),
        ]
        scratch = [
            ((rows, D), F32), ((rows, D), BF), ((rows, FF), BF), ((rows, FF), F32), ((rows, D), F32),
            ((rows, D), BF), ((rows, FF), BF),
        ]
        return call(body, "turn", outs, scratch, meta, h, o, vec, proj_w, fc1_w, fc2_w, cot)

    return run


def mlp_back(seqs, slots, total):
    rows = total * TILE

    def body(meta, g, mid, a2, act, slope, vec, fc1_w, fc2_w, proj_w, grads, small, g1, dp, do, dm, du):
        tiles = meta[2 * seqs]
        small[...] = jnp.zeros_like(small)
        phase_mlp_back(tiles, g, mid, slope, vec, fc1_w, fc2_w, proj_w, dm, du, g1, dp, do, small)
        zero_tail(tiles, total, [dm, du, dp, do])
        outer_products(tiles, total, [(du, a2, store_rows(grads, 0)), (act, dm, store_rows(grads, FF))])

    def run(meta, *args):
        outs = [((2 * FF, D), BF), ((8, FF), F32), ((rows, D), F32), ((rows, D), BF), ((rows, D), BF)]
        return call(body, "mlp_back", outs, [((rows, D), BF), ((rows, FF), BF)], meta, *args)

    return run


def attn_back(seqs, slots, total, last):
    rows = total * TILE

    def body(meta, h, qkv, lse, do, a1, o, dp, g1, vec, qkv_w, grads, small, g_out, dqkv, g_flat):
        tiles = meta[2 * seqs]
        small[...] = jnp.zeros_like(small)
        dqkv[...] = jnp.zeros_like(dqkv)
        attend_back(meta, seqs, slots, qkv, do, lse, dqkv)
        packed = g_flat if last else g_out
        phase_qkv_back(tiles, h, g1, dqkv, vec, qkv_w, packed, small)
        outer_products(tiles, total, [(dqkv, a1, store_rows(grads, 0)), (dp, o, store_rows(grads, 3 * D))])
        if last:
            for i in range(seqs):
                at = pl.multiple_of(meta[seqs + i], 16)
                keep = lax.broadcasted_iota(jnp.int32, (slots, D), 0) < meta[i]
                g_out[i] = jnp.where(keep, packed[pl.ds(at, slots), :], 0.0)

    def run(meta, *args):
        g_shape = (seqs, slots, D) if last else (rows, D)
        outs = [((4 * D, D), BF), ((8, FF), F32), (g_shape, F32)]
        flat = (rows, D) if last else (8, D)
        return call(body, "attn_back_last" if last else "attn_back", outs, [((rows, 3 * D), BF), (flat, F32)], meta, *args)

    return run


FAST = {"dp": 8, "tok": 4}
GATHER = (("dp", 2), ("dp", 4), ("dp", 1), ("tok", 2), ("tok", 1))


def swap(x, axis, bit):
    size = lax.axis_size(axis)
    return lax.ppermute(x, axis, [(i, i ^ bit) for i in range(size)])


def upper(axis, bit):
    return (lax.axis_index(axis) & bit) != 0


def gather_blocks(piece, steps=GATHER):
    cur = piece
    for axis, bit in steps:
        other = swap(cur, axis, bit)
        high = upper(axis, bit)
        cur = jnp.stack([jnp.where(high, other, cur), jnp.where(high, cur, other)])
    return cur


def scatter_blocks(blocks, steps=GATHER[::-1]):
    cur = blocks
    for axis, bit in steps:
        high = upper(axis, bit)
        mine = jnp.where(high, cur[1], cur[0]).astype(F32)
        away = jnp.where(high, cur[0], cur[1]).astype(BF)
        cur = mine + swap(away, axis, bit).astype(F32)
    return cur


def by_shard(full):
    full = full.transpose(0, 1, 3, 4, 2, 5, 6)
    return full.reshape(4, 8, full.shape[-2], D)


def from_shard(blocks):
    return blocks.reshape(2, 2, 2, 2, 2, blocks.shape[-2], D).transpose(0, 1, 4, 2, 3, 5, 6)


def own_quarter(shard):
    tok = lax.axis_index("tok")
    quarter = (tok % 2) * 2 + tok // 2
    rows = shard.shape[0] // 4
    return lax.dynamic_slice_in_dim(shard, quarter * rows, rows, 0)


def gather_fast(att, mlp):
    att_all = by_shard(gather_blocks(own_quarter(att)))
    mlp_all = by_shard(gather_blocks(own_quarter(mlp)))
    qkv = att_all[0:3].transpose(1, 0, 2, 3).reshape(3 * D, D)
    proj = att_all[3].reshape(D, D)
    up = mlp_all[0:2].transpose(1, 0, 2, 3).reshape(FF, D)
    down = mlp_all[2:4].transpose(1, 0, 2, 3).reshape(FF, D)
    return qkv, proj, up, down


def tok_gather(part):
    full = gather_blocks(part.astype(BF), GATHER[3:])
    return full.reshape(-1, D).astype(F32)


def scatter_mlp_fast(grads):
    up = grads[0:FF].reshape(8, 2, -1, D).transpose(1, 0, 2, 3)
    down = grads[FF:].reshape(8, 2, -1, D).transpose(1, 0, 2, 3)
    full = tok_gather(scatter_blocks(from_shard(jnp.concatenate([up, down]))))
    return full[0 : FF // 8], full[FF // 8 :]


def scatter_att_fast(grads):
    qkv = grads[0 : 3 * D].reshape(8, 3, -1, D).transpose(1, 0, 2, 3)
    proj = grads[3 * D :].reshape(1, 8, -1, D)
    full = tok_gather(scatter_blocks(from_shard(jnp.concatenate([qkv, proj]))))
    return full[0 : 3 * D // 8], full[3 * D // 8 :]


def gather_any(att, mlp):
    def whole(rows):
        return lax.all_gather(rows, "dp", axis=0, tiled=True)

    wide = att.shape[0] * 3 // 4
    half = mlp.shape[0] // 2
    return whole(att[:wide]), whole(att[wide:]), whole(mlp[:half]), whole(mlp[half:])


def scatter_any(grads, cut):
    def part(rows):
        return lax.psum(lax.psum_scatter(rows.astype(F32), "dp", scatter_dimension=0, tiled=True), "tok")

    return part(grads[:cut]), part(grads[cut:])


def sum_all_fast(x, steps):
    for axis, bit in steps:
        x = x + swap(x, axis, bit)
    return x


def adamw(weight, moments, clipped, rate, decay):
    first_mom = 0.9 * moments[0] + 0.1 * clipped
    second_mom = 0.999 * moments[1] + 0.001 * clipped * clipped
    fixed_first = first_mom / (1.0 - 0.9**STEP)
    fixed_second = second_mom / (1.0 - 0.999**STEP)
    new_weight = weight - rate * (fixed_first / (jnp.sqrt(fixed_second) + 1e-08) + decay * weight)
    return (jnp.stack([new_weight, first_mom]), second_mom)


def small_rows(gains, biases):
    gains, biases = gains.astype(F32), biases.astype(F32)

    def row(*parts):
        flat = jnp.concatenate(parts)
        return jnp.pad(flat, (0, FF - flat.shape[0]))

    cut = [biases[i * D : (i + 1) * D] for i in range(6)]
    qkv = row(cut[1], jnp.zeros((D,), F32), cut[2])
    return jnp.stack([row(gains[0]), row(cut[0]), row(gains[1]), row(cut[4]), row(cut[3]), row(cut[5]), biases[6 * D :], qkv])


def small_back(rows):
    gains = jnp.stack([rows[0, :D], rows[2, :D]])
    biases = jnp.concatenate([rows[1, :D], rows[7, :D], rows[7, 2 * D : 3 * D], rows[4, :D], rows[3, :D], rows[5, :D], rows[6]])
    return gains, biases


def on_device(x, cot, lengths, w_qkv, w_proj, w_fc1, w_fc2, norm_gains, biases,
              mom_qkv, mom_proj, mom_fc1, mom_fc2, mom_gains, mom_biases):
    fast = all(lax.axis_size(a) == n for a, n in FAST.items())
    seqs, slots = x.shape[0], x.shape[1]
    own = lax.dynamic_slice_in_dim(lengths, lax.axis_index("tok") * seqs, seqs, 0)
    meta = plan_rows(own, slots)
    total = packed_tiles(seqs, slots)
    size = (seqs, slots, total)
    att = [jnp.concatenate([w_qkv[l].T, w_proj[l].T]).astype(BF) for l in range(LAYERS)]
    mlp = [jnp.concatenate([w_fc1[l].T, w_fc2[l]]).astype(BF) for l in range(LAYERS)]
    small = jnp.concatenate([norm_gains.reshape(LAYERS, -1), biases], 1).astype(BF)
    gather = gather_fast if fast else gather_any
    if fast:
        small = gather_blocks(small, GATHER[:3]).transpose(1, 2, 0, 3, 4).reshape(-1, *small.shape)
    else:
        small = lax.all_gather(small, "dp")
    shards = small.shape[0]
    cut = 2 * D // shards
    gains_all = small[:, :, :cut].reshape(shards, LAYERS, 2, -1).transpose(1, 2, 0, 3).reshape(LAYERS, 2, D)
    biases_all = small[:, :, cut:].transpose(1, 0, 2).reshape(LAYERS, -1)
    vecs = [small_rows(gains_all[l], biases_all[l]) for l in range(LAYERS)]
    qkv0, proj0, up0, down0 = gather(att[0], mlp[0])
    qkv1, proj1, up1, down1 = gather(att[1], mlp[1])
    h0, a0, p0, o0, lse0 = first_half(*size)(meta, x, vecs[0], qkv0)
    mid0, b0, act0, slope0, h1, a1, p1, o1, lse1 = middle(*size)(
        meta, h0, o0, vecs[0], proj0, up0, down0, vecs[1], qkv1
    )
    layer_out, mlp1, small1a, g1, dp1, do1 = turn(*size)(meta, h1, o1, vecs[1], proj1, up1, down1, cot)
    scatter_mlp = scatter_mlp_fast if fast else (lambda g: scatter_any(g, FF))
    scatter_att = scatter_att_fast if fast else (lambda g: scatter_any(g, 3 * D))
    att1, small1b, g = attn_back(*size, False)(meta, h1, p1, lse1, do1, a1, o1, dp1, g1, vecs[1], qkv1)
    mlp0, small0a, g1, dp0, do0 = mlp_back(*size)(meta, g, mid0, b0, act0, slope0, vecs[0], up0, down0, proj0)
    att0, small0b, input_grad = attn_back(*size, True)(
        meta, h0, p0, lse0, do0, a0, o0, dp0, g1, vecs[0], qkv0
    )
    up_g1, down_g1 = scatter_mlp(mlp1)
    qkv_g1, proj_g1 = scatter_att(att1)
    up_g0, down_g0 = scatter_mlp(mlp0)
    qkv_g0, proj_g0 = scatter_att(att0)
    smalls = jnp.stack([small0a + small0b, small1a + small1b])
    smalls = sum_all_fast(smalls, GATHER) if fast else lax.psum(smalls, ("dp", "tok"))
    grads = [
        jnp.stack([qkv_g0.T, qkv_g1.T]),
        jnp.stack([proj_g0.T, proj_g1.T]),
        jnp.stack([up_g0.T, up_g1.T]),
        jnp.stack([down_g0, down_g1]),
    ]
    gains_g, biases_g = (jnp.stack(t) for t in zip(*(small_back(smalls[l]) for l in range(LAYERS))))
    squares = sum(jnp.sum(g * g) for g in grads)
    squares = sum_all_fast(squares, GATHER[:3]) if fast else lax.psum(squares, "dp")
    squares = squares + jnp.sum(gains_g * gains_g) + jnp.sum(biases_g * biases_g)
    dp_index = lax.axis_index("dp")
    grads.append(lax.dynamic_slice_in_dim(gains_g, dp_index * norm_gains.shape[2], norm_gains.shape[2], 2))
    grads.append(lax.dynamic_slice_in_dim(biases_g, dp_index * biases.shape[1], biases.shape[1], 1))
    grad_norm = jnp.sqrt(squares)
    limit = 0.25 * math.sqrt(LAYERS * (4 * D * D + 2 * D * FF + 8 * D + FF))
    factor = jnp.minimum(1.0, limit / (grad_norm + 1e-06))
    masters = (w_qkv, w_proj, w_fc1, w_fc2, norm_gains, biases)
    moments = (mom_qkv, mom_proj, mom_fc1, mom_fc2, mom_gains, mom_biases)
    states, seconds = [], []
    for index in range(6):
        rate, decay = (0.08, 0.05) if index < 4 else (0.4, 0.0)
        state, second = adamw(masters[index], moments[index], grads[index] * factor, rate, decay)
        states.append(state)
        seconds.append(second.reshape(-1))
    return (layer_out, input_grad, grad_norm, *states, jnp.concatenate(seconds))


def solution(mesh):
    rows = P(("dp", "tok"), None, None)
    weights = (P(None, None, "dp"),) * 3 + (P(None, "dp", None), P(None, None, "dp"), P(None, "dp"))
    stacked = tuple(P(None, *spec) for spec in weights)
    return jax.shard_map(
        on_device,
        mesh=mesh,
        in_specs=(rows, rows, P("dp"), *weights, *stacked),
        out_specs=(rows, rows, P(), *stacked, P("dp")),
        check_vma=False,
    )
```

```python
import functools
import math

import jax
import jax.numpy as jnp
from jax import lax
from jax.experimental import pallas as pl
from jax.experimental.pallas import tpu as pltpu
from jax.sharding import PartitionSpec as P

D = 384
HEADS = 6
HD = 64
FF = 1536
LAYERS = 2
STEP = 10
PAIRS = HEADS // 2
TILE = 128
BIG = 256
EPS = 1e-06
HALF_ROOT = 0.7071067811865476
INV_ROOT_TAU = 0.3989422804014327
LOG2E = 1.4426950408889634
SCORE = 0.125 * LOG2E
TAIL_P = 0.4
TAIL = (
    0.22480539044849576,
    0.2382192213985389,
    0.13072083829499273,
    0.43284363894582684,
    -0.41172890451981375,
    0.7191256145749827,
    -0.41194367033429247,
    0.07795786677173361,
)
BF = jnp.bfloat16
F32 = jnp.float32


def nn(a, b):
    return lax.dot_general(a, b, (((1,), (0,)), ((), ())), preferred_element_type=F32)


def nt(a, b):
    return lax.dot_general(a, b, (((1,), (1,)), ((), ())), preferred_element_type=F32)


def tn(a, b):
    return lax.dot_general(a, b, (((0,), (0,)), ((), ())), preferred_element_type=F32)


def normalize(hidden):
    centered = hidden - jnp.mean(hidden, -1, keepdims=True)
    variance = jnp.mean(centered * centered, -1, keepdims=True)
    inverse = lax.rsqrt(variance + EPS)
    return centered * inverse, inverse


def norm_back(grad_n, normed, inverse):
    first = jnp.mean(grad_n, -1, keepdims=True)
    second = jnp.mean(grad_n * normed, -1, keepdims=True)
    return inverse * (grad_n - first - normed * second)


def gelu_pair(u):
    t = 1.0 / (1.0 + (TAIL_P * HALF_ROOT) * jnp.abs(u))
    bell = jnp.exp2(u * u * (-0.5 * LOG2E))
    poly = jnp.full_like(t, 0.5 * TAIL[-1])
    for coef in TAIL[-2::-1]:
        poly = poly * t + 0.5 * coef
    low = poly * t * bell
    cdf = jnp.where(u < 0.0, low, 1.0 - low)
    return u * cdf, cdf + u * bell * INV_ROOT_TAU


def both_heads(x):
    lane = lax.broadcasted_iota(jnp.int32, x.shape, 1)
    zero = jnp.zeros_like(x)
    return jnp.concatenate([jnp.where(lane < HD, x, zero), jnp.where(lane >= HD, x, zero)], 0)


def pick(both):
    half = both.shape[0] // 2
    lane = lax.broadcasted_iota(jnp.int32, (half, 2 * HD), 1)
    return jnp.where(lane < HD, both[:half], both[half:])


QB = 128


def by_length(meta, seqs, slots, run):
    full = -(-slots // 16) * 16
    sizes = [(w, -(-w // QB)) for w in (64, 128, 160) if w < full] + [(full, -(-full // QB))]

    def body(i, carry):
        length, start = meta[i], pl.multiple_of(meta[seqs + i], 16)
        low = 0
        for keys, blocks in sizes:
            pl.when(jnp.logical_and(length > low, length <= keys))(
                functools.partial(run, i, start, length, keys, blocks)
            )
            low = keys
        return carry

    lax.fori_loop(0, seqs, body, 0)


def attend(meta, seqs, slots, qkv_ref, o_ref, lse_ref):
    def run(i, start, length, keys, blocks):
        rows = pl.ds(start, keys)
        keep = lax.broadcasted_iota(jnp.int32, (keys, 2 * QB), 0) < length
        for pair in range(PAIRS):
            at = pair * 2 * HD
            k = qkv_ref[rows, D + at : D + at + 2 * HD]
            v = qkv_ref[rows, 2 * D + at : 2 * D + at + 2 * HD]
            for block in range(blocks):
                part = pl.ds(start + block * QB, QB)
                q = both_heads(qkv_ref[part, at : at + 2 * HD])
                s = jnp.where(keep, nt(k, q), -1e30)
                top = jnp.max(s, 0, keepdims=True)
                e = jnp.exp2((s - top) * SCORE)
                total = jnp.sum(e, 0, keepdims=True)
                p = (e * (1.0 / total)).astype(BF)
                o_ref[part, at : at + 2 * HD] = pick(tn(p, v)).astype(BF)
                lse_ref[i, pair : pair + 1, block * 2 * QB : (block + 1) * 2 * QB] = top * SCORE + jnp.log2(total)

    by_length(meta, seqs, slots, run)


def attend_back(meta, seqs, slots, qkv_ref, do_ref, lse_ref, dqkv_ref):
    def run(i, start, length, keys, blocks):
        rows = pl.ds(start, keys)
        keep = lax.broadcasted_iota(jnp.int32, (keys, 2 * QB), 0) < length
        for pair in range(PAIRS):
            at = pair * 2 * HD
            k = qkv_ref[rows, D + at : D + at + 2 * HD]
            v = qkv_ref[rows, 2 * D + at : 2 * D + at + 2 * HD]
            dk, dv = 0.0, 0.0
            for block in range(blocks):
                part = pl.ds(start + block * QB, QB)
                q = both_heads(qkv_ref[part, at : at + 2 * HD])
                do = do_ref[part, at : at + 2 * HD]
                row = lax.broadcasted_iota(jnp.int32, do.shape, 0)
                do = both_heads(jnp.where(row < length - block * QB, do, jnp.zeros_like(do)))
                lse = lse_ref[i, pair : pair + 1, block * 2 * QB : (block + 1) * 2 * QB]
                p = jnp.where(keep, jnp.exp2(nt(k, q) * SCORE - lse), 0.0)
                dp = nt(v, do)
                inner = jnp.sum(p * dp, 0, keepdims=True)
                ds = (p * (dp - inner)).astype(BF)
                dv = dv + nn(p.astype(BF), do)
                dk = dk + nn(ds, q)
                dqkv_ref[part, at : at + 2 * HD] = (pick(tn(ds, k)) * 0.125).astype(BF)
            dqkv_ref[rows, D + at : D + at + 2 * HD] = (dk * 0.125).astype(BF)
            dqkv_ref[rows, 2 * D + at : 2 * D + at + 2 * HD] = dv.astype(BF)

    by_length(meta, seqs, slots, run)


def over_rows(tiles, body):
    def step(t, carry):
        body(pl.ds(pl.multiple_of(t * BIG, BIG), BIG))
        return carry

    lax.fori_loop(0, tiles // 2, step, 0)
    odd = tiles % 2 == 1
    pl.when(odd)(lambda: body(pl.ds(pl.multiple_of((tiles - 1) * TILE, TILE), TILE)))


def zero_tail(tiles, total, refs):
    def body(t, carry):
        rows = pl.ds(pl.multiple_of(t * TILE, TILE), TILE)
        for ref in refs:
            ref[rows, :] = jnp.zeros((TILE, ref.shape[1]), ref.dtype)
        return carry

    lax.fori_loop(tiles, total, body, 0)


B_LN1, B_Q, B_V, B_PROJ, B_LN2, B_2, B_1, GAIN1, GAIN2 = 0, 1, 2, 3, 4, 5, 6, 10, 11
SMALL = 16


def row(ref, index, count=1):
    return jnp.concatenate([ref[index + i : index + i + 1, :] for i in range(count)], 1)


def add_row(ref, index, value):
    total = jnp.sum(value, 0, keepdims=True)
    for i in range(value.shape[1] // D):
        ref[index + i : index + i + 1, :] += total[:, i * D : (i + 1) * D]


def phase_qkv(tiles, h_ref, vec, att_w, a_ref, qkv_ref):
    def body(rows):
        normed, _ = normalize(h_ref[rows, :])
        a = (normed * row(vec, GAIN1) + row(vec, B_LN1)).astype(BF)
        a_ref[rows, :] = a
        bias = jnp.concatenate([row(vec, B_Q), jnp.zeros((1, D), F32), row(vec, B_V)], 1)
        qkv_ref[rows, :] = (nt(a, att_w[0 : 3 * D, :]) + bias).astype(BF)

    over_rows(tiles, body)


def phase_mlp(tiles, h_ref, o_ref, vec, att_w, mlp_w, mid_ref, a_ref, act_ref, slope_ref, out_ref):
    wide = 2 * D

    def body(rows):
        mid = h_ref[rows, :] + nt(o_ref[rows, :], att_w[3 * D :, :]) + row(vec, B_PROJ)
        mid_ref[rows, :] = mid
        normed, _ = normalize(mid)
        a = (normed * row(vec, GAIN2) + row(vec, B_LN2)).astype(BF)
        a_ref[rows, :] = a
        for c in range(0, FF, wide):
            u = nt(a, mlp_w[c : c + wide, :]) + row(vec, B_1 + c // D, wide // D)
            act, slope = gelu_pair(u)
            act_ref[rows, c : c + wide] = act.astype(BF)
            slope_ref[rows, c : c + wide] = slope
        out_ref[rows, :] = mid + nn(act_ref[rows, :], mlp_w[FF:, :]) + row(vec, B_2)

    over_rows(tiles, body)


def phase_mlp_back(tiles, g_ref, mid_ref, slope_ref, vec, att_w, mlp_w, dm_ref, du_ref, g1_ref, dp_ref, do_ref, small):
    wide = 2 * D

    def body(rows):
        g = g_ref[rows, :]
        dm = g.astype(BF)
        dm_ref[rows, :] = dm
        add_row(small, B_2, dm.astype(F32))
        for c in range(0, FF, wide):
            du = (nt(dm, mlp_w[FF + c : FF + c + wide, :]) * slope_ref[rows, c : c + wide]).astype(BF)
            du_ref[rows, c : c + wide] = du
            add_row(small, B_1 + c // D, du.astype(F32))
        da = nn(du_ref[rows, :], mlp_w[0:FF, :])
        normed, inverse = normalize(mid_ref[rows, :])
        add_row(small, GAIN2, da * normed)
        add_row(small, B_LN2, da)
        g1 = g + norm_back(da * row(vec, GAIN2), normed, inverse)
        g1_ref[rows, :] = g1
        dp = g1.astype(BF)
        dp_ref[rows, :] = dp
        add_row(small, B_PROJ, dp.astype(F32))
        do_ref[rows, :] = nn(dp, att_w[3 * D :, :]).astype(BF)

    over_rows(tiles, body)


def phase_qkv_back(tiles, h_ref, g1_ref, dqkv_ref, vec, att_w, g_out, small):
    def body(rows):
        dqkv = dqkv_ref[rows, :]
        add_row(small, B_Q, dqkv[:, 0:D].astype(F32))
        add_row(small, B_V, dqkv[:, 2 * D :].astype(F32))
        da = nn(dqkv, att_w[0 : 3 * D, :])
        normed, inverse = normalize(h_ref[rows, :])
        add_row(small, GAIN1, da * normed)
        add_row(small, B_LN1, da)
        g_out[rows, :] = g1_ref[rows, :] + norm_back(da * row(vec, GAIN1), normed, inverse)

    over_rows(tiles, body)


def outer_products(tiles, total, jobs):
    wide, low = 3 * 128, 0
    for size in sorted(set(min(k, total) for k in (3, 4, 5, 6, total))):

        def run(size=size):
            rows = size * TILE
            for left, right, result in jobs:
                for m in range(0, left.shape[1], wide):
                    result[m : m + wide, :] = tn(left[0:rows, m : m + wide], right[0:rows, :]).astype(result.dtype)

        pl.when(jnp.logical_and(tiles > low, tiles <= size))(run)
        low = size


def on_chip(shape, dtype):
    return pltpu.VMEM(shape, dtype)


def anywhere(shape, dtype):
    return jax.ShapeDtypeStruct(shape, dtype)


def call(body, name, outs, scratch, us, *arrays):
    specs, placed = [], []
    for a in arrays:
        if a.dtype == jnp.int32:
            specs.append(pl.BlockSpec(memory_space=pltpu.SMEM))
            placed.append(a)
        else:
            specs.append(pl.BlockSpec(memory_space=pltpu.VMEM))
            placed.append(pltpu.with_memory_space_constraint(a, pltpu.VMEM) if a.ndim == 2 else a)
    return pl.pallas_call(
        body,
        name=name,
        out_shape=list(outs),
        in_specs=specs,
        out_specs=[pl.BlockSpec(memory_space=pltpu.VMEM)] * len(outs),
        scratch_shapes=list(scratch),
        compiler_params=pltpu.CompilerParams(vmem_limit_bytes=16 << 20),
        cost_estimate=pl.CostEstimate(flops=int(us * 1e9), bytes_accessed=0, transcendentals=0),
    )(*placed)


def plan_rows(lengths):
    room = (lengths + 15) // 16 * 16
    ends = jnp.cumsum(room)
    tiles = (ends[-1:] + TILE - 1) // TILE
    return jnp.concatenate([lengths, ends - room, tiles]).astype(jnp.int32)


def packed_tiles(seqs, slots):
    full = -(-slots // 16) * 16
    return -(-(seqs * full) // TILE)


class Kernels:
    def __init__(self, meta, seqs, slots):
        self.meta, self.seqs, self.slots = meta, seqs, slots
        self.total = packed_tiles(seqs, slots)
        self.rows = self.total * TILE

    def wide(self, width, dtype):
        return on_chip((self.rows, width), dtype)

    def lse(self):
        return on_chip((self.seqs, 8, -(-self.slots // QB) * 2 * QB), F32)

    def tiles(self, meta):
        return meta[2 * self.seqs]

    def spans(self, meta):
        for i in range(self.seqs):
            start = pl.multiple_of(meta[self.seqs + i], 16)
            keep = lax.broadcasted_iota(jnp.int32, (self.slots, D), 0) < meta[i]
            yield i, pl.ds(start, self.slots), keep

    def qkv_first(self, x, vec, att_w):
        def body(meta, x_ref, vec, att_w, h, a, qkv):
            h[...] = jnp.zeros_like(h)
            for i, rows, _ in self.spans(meta):
                h[rows, :] = x_ref[i].astype(F32)
            phase_qkv(self.tiles(meta), h, vec, att_w, a, qkv)
            zero_tail(self.tiles(meta), self.total, [a, qkv])

        outs = [self.wide(D, F32), self.wide(D, BF), self.wide(3 * D, BF)]
        return call(body, "qkv_first", outs, [], 2.5, self.meta, x, vec, att_w)

    def qkv(self, h, vec, att_w):
        def body(meta, h, vec, att_w, a, qkv):
            phase_qkv(self.tiles(meta), h, vec, att_w, a, qkv)
            zero_tail(self.tiles(meta), self.total, [a, qkv])

        return call(body, "qkv", [self.wide(D, BF), self.wide(3 * D, BF)], [], 2, self.meta, h, vec, att_w)

    def attend(self, qkv):
        def body(meta, qkv, o, lse):
            o[...] = jnp.zeros_like(o)
            lse[...] = jnp.zeros_like(lse)
            attend(meta, self.seqs, self.slots, qkv, o, lse)

        return call(body, "attend", [self.wide(D, BF), self.lse()], [], 4, self.meta, qkv)

    def mlp(self, h, o, vec, att_w, mlp_w):
        def body(meta, h, o, vec, att_w, mlp_w, mid, a, act, slope, out):
            phase_mlp(self.tiles(meta), h, o, vec, att_w, mlp_w, mid, a, act, slope, out)
            zero_tail(self.tiles(meta), self.total, [a, act])

        outs = [self.wide(D, F32), self.wide(D, BF), self.wide(FF, BF), self.wide(FF, F32), self.wide(D, F32)]
        return call(body, "mlp", outs, [], 6, self.meta, h, o, vec, att_w, mlp_w)

    def finish(self, h, cot):
        def body(meta, h, cot, out, g):
            g[...] = jnp.zeros_like(g)
            for i, rows, keep in self.spans(meta):
                out[i] = jnp.where(keep, h[rows, :], 0.0).astype(BF)
                g[rows, :] = jnp.where(keep, cot[i].astype(F32), 0.0)

        return call(body, "finish", [anywhere(cot.shape, BF), self.wide(D, F32)], [], 1, self.meta, h, cot)

    def mlp_back(self, g, mid, slope, vec, att_w, mlp_w):
        def body(meta, g, mid, slope, vec, att_w, mlp_w, dm, du, g1, dp, do, small):
            small[...] = jnp.zeros_like(small)
            phase_mlp_back(self.tiles(meta), g, mid, slope, vec, att_w, mlp_w, dm, du, g1, dp, do, small)
            zero_tail(self.tiles(meta), self.total, [dm, du, dp, do])

        outs = [self.wide(D, BF), self.wide(FF, BF), self.wide(D, F32), self.wide(D, BF), self.wide(D, BF)]
        outs.append(on_chip((SMALL, D), F32))
        return call(body, "mlp_back", outs, [], 4, self.meta, g, mid, slope, vec, att_w, mlp_w)

    def attend_back(self, qkv, do, lse):
        def body(meta, qkv, do, lse, dqkv):
            dqkv[...] = jnp.zeros_like(dqkv)
            attend_back(meta, self.seqs, self.slots, qkv, do, lse, dqkv)

        return call(body, "attend_back", [self.wide(3 * D, BF)], [], 6, self.meta, qkv, do, lse)[0]

    def qkv_back(self, h, g1, dqkv, vec, att_w):
        def body(meta, h, g1, dqkv, vec, att_w, g, small):
            small[...] = jnp.zeros_like(small)
            phase_qkv_back(self.tiles(meta), h, g1, dqkv, vec, att_w, g, small)

        outs = [self.wide(D, F32), on_chip((SMALL, D), F32)]
        return call(body, "qkv_back", outs, [], 2, self.meta, h, g1, dqkv, vec, att_w)

    def unpack(self, g):
        def body(meta, g, out):
            for i, rows, keep in self.spans(meta):
                out[i] = jnp.where(keep, g[rows, :], 0.0)

        return call(body, "unpack", [anywhere((self.seqs, self.slots, D), F32)], [], 1, self.meta, g)[0]

    def outer(self, name, pairs, parts=None, smalls=()):
        height = sum(left.shape[1] for left, _ in pairs)
        count = len(pairs)

        def products(meta, refs, result):
            jobs, base = [], 0
            for i in range(count):
                left, right = refs[2 * i], refs[2 * i + 1]
                jobs.append((left, right, result.at[base : base + left.shape[1]]))
                base += left.shape[1]
            outer_products(self.tiles(meta), self.total, jobs)

        flat = [a for pair in pairs for a in pair]
        if parts is None:
            def body(meta, *refs):
                products(meta, refs, refs[-1])

            return call(body, name, [on_chip((height, D), BF)], [], 2, self.meta, *flat)[0]

        extra = 8 if smalls else 0
        size = height // 16

        def body(meta, pos, *refs):
            small_refs = refs[2 * count : 2 * count + len(smalls)]
            outs, result = refs[2 * count + len(smalls) : 2 * count + len(smalls) + 4], refs[-1 - (extra > 0)]
            products(meta, refs, result)
            if extra:
                held = refs[-1]
                held[...] = jnp.zeros_like(held)
                for layer in range(LAYERS):
                    own = small_refs[2 * layer][...] + small_refs[2 * layer + 1][...]
                    for d in range(8):
                        held[layer, d, 0:2, :] = own[2 * d : 2 * d + 2, :]
            for out, side, x_rel in zip(outs, (0, 0, 1, 1), (0, 1, 0, 1)):
                for z_rel in range(4):
                    shard, half, pieces = parts(pos, side, x_rel, z_rel)
                    for at, source, n in pieces:
                        out[z_rel, at : at + n, :] = result[pl.ds(source, n), :]
                    if extra:
                        out[z_rel, size : size + extra, :] = held[half, shard].astype(BF)

        outs = [anywhere((4, size + extra, D), BF)] * 4
        scratch = [on_chip((height, D), BF)] + ([on_chip((LAYERS, 8, 8, D), F32)] if extra else [])
        return call(body, name, outs, scratch, 3, self.meta, parts.pos, *flat, *smalls)


def swap(x, axis, bit):
    return lax.ppermute(x, axis, [(i, i ^ bit) for i in range(lax.axis_size(axis))])


def fast_mesh():
    return lax.axis_size("dp") == 8 and lax.axis_size("tok") == 4


class Place:
    def __init__(self):
        dp, tok = lax.axis_index("dp"), lax.axis_index("tok")
        self.z, self.x, self.core = dp // 2, dp % 2, tok % 2
        self.pos = jnp.stack([self.z, self.x, self.core]).astype(jnp.int32)


def block_rows(kind, pos, side, x_rel, z_rel):
    shard = (pos[0] ^ z_rel) * 2 + (pos[1] ^ x_rel)
    half = pos[2] ^ side
    if kind == "mlp":
        return shard, half, [(0, pl.multiple_of(half * FF + shard * (FF // 8), 16), FF // 8)]
    n = D // 8
    pieces = []
    for s in range(2):
        u = half * 2 + s
        source = jnp.where(u < 3, shard * 3 * n + u * n, 3 * D + shard * n)
        pieces.append((s * n, pl.multiple_of(source, 16), n))
    return shard, half, pieces


class Parts:
    def __init__(self, kind, pos):
        self.kind, self.pos = kind, pos

    def __call__(self, pos, side, x_rel, z_rel):
        return block_rows(self.kind, pos, side, x_rel, z_rel)


def assemble(kind, pos, blocks, with_small):
    size = 2 * D // 16 * 2 if kind == "att" else FF // 8
    height = 4 * D if kind == "att" else 2 * FF

    def body(pos, *refs):
        blocks, out = refs[:4], refs[4]
        for block, side, x_rel in zip(blocks, (0, 0, 1, 1), (0, 1, 0, 1)):
            for z_rel in range(4):
                _, _, pieces = block_rows(kind, pos, side, x_rel, z_rel)
                for at, target, n in pieces:
                    out[pl.ds(target, n), :] = block[z_rel, at : at + n, :]
        if with_small:
            for vec in refs[5:]:
                vec[...] = jnp.zeros_like(vec)
            for shard in range(8):
                z_rel = pos[0] ^ (shard // 2)
                near = blocks[0][z_rel, size : size + 8, :].astype(F32)
                far = blocks[1][z_rel, size : size + 8, :].astype(F32)
                rows = jnp.where(pos[1] == shard % 2, near, far)
                first = shard * 10 // 8
                for layer in range(LAYERS):
                    vec, base = refs[5 + layer], 4 * layer
                    vec[first : first + 2, :] += rows[base : base + 2, :]
                    vec[GAIN1 : GAIN1 + 2, :] += rows[base + 2 : base + 4, :]

    outs = [on_chip((height, D), BF)] + [on_chip((SMALL, D), F32)] * (LAYERS if with_small else 0)
    return call(body, "assemble_" + kind, outs, [], 1, pos, *blocks)


def spread_small(gains, biases, shard):
    out = []
    for layer in range(LAYERS):
        bias = lax.dynamic_update_slice(jnp.zeros((2 * D,), F32), biases[layer], (shard * (10 * D // 8) % D,))
        gain = lax.dynamic_update_slice(jnp.zeros((2, D), F32), gains[layer], (0, shard * (D // 8)))
        out += [bias.reshape(2, D), gain]
    return jnp.concatenate(out)


def gather_blocks(piece):
    near = jnp.stack([piece] + [swap(piece, "dp", 2 * k) for k in (1, 2, 3)])
    far = swap(near, "dp", 1)
    return near, far, swap(near, "tok", 1), swap(far, "tok", 1)


def scatter_blocks(keep_near, keep_far, send_near, send_far):
    other_far = swap(send_far, "tok", 1)
    away = (keep_far.astype(F32) + other_far.astype(F32)).astype(BF)
    other_near = swap(send_near, "tok", 1)
    back = swap(away, "dp", 1)
    near = keep_near.astype(F32) + other_near.astype(F32) + back.astype(F32)
    low = near.astype(BF)
    mine = near[0] + sum(swap(low[k], "dp", 2 * k).astype(F32) for k in (1, 2, 3))
    mine = mine.astype(BF)
    mine = (mine.astype(F32) + swap(mine, "tok", 2).astype(F32)).astype(BF)
    return mine, swap(mine, "tok", 1)


def in_order(core, mine, other):
    return jnp.where(core == 0, jnp.concatenate([mine, other]), jnp.concatenate([other, mine])).astype(F32)


def sum_chips(x):
    x = (x + swap(x, "dp", 2)) + (swap(x, "dp", 4) + swap(x, "dp", 6))
    return x + swap(x, "dp", 1)


def adamw(weight, moments, clipped, rate, decay):
    first_mom = 0.9 * moments[0] + 0.1 * clipped
    second_mom = 0.999 * moments[1] + 0.001 * clipped * clipped
    fixed_first = first_mom / (1.0 - 0.9**STEP)
    fixed_second = second_mom / (1.0 - 0.999**STEP)
    new_weight = weight - rate * (fixed_first / (jnp.sqrt(fixed_second) + 1e-08) + decay * weight)
    return (jnp.stack([new_weight, first_mom]), second_mom)


def whole_small(gains, biases):
    rows = jnp.concatenate([biases.reshape(10, D), gains]).astype(F32)
    return jnp.pad(rows, ((0, SMALL - 12), (0, 0)))


def on_device(x, cot, lengths, w_qkv, w_proj, w_fc1, w_fc2, norm_gains, biases,
              mom_qkv, mom_proj, mom_fc1, mom_fc2, mom_gains, mom_biases):
    fast = fast_mesh()
    seqs, slots = x.shape[0], x.shape[1]
    own = lax.dynamic_slice_in_dim(lengths, lax.axis_index("tok") * seqs, seqs, 0)
    k = Kernels(plan_rows(own), seqs, slots)
    dp_index = lax.axis_index("dp")
    if fast:
        place = Place()
        att_parts, mlp_parts = Parts("att", place.pos), Parts("mlp", place.pos)

        def half(rows):
            size = rows.shape[0] // 2
            return lax.dynamic_slice_in_dim(rows, place.core * size, size, 0)

        small = spread_small(norm_gains, biases, dp_index)
        att = [half(jnp.concatenate([w_qkv[l].T, w_proj[l].T])) for l in range(LAYERS)]
        mlp = [jnp.where(place.core == 0, w_fc1[l].T, w_fc2[l]) for l in range(LAYERS)]
        first = jnp.concatenate([att[0], small]).astype(BF)
        att_w0, vec0, vec1 = assemble("att", place.pos, gather_blocks(first), True)
        mlp_w0, = assemble("mlp", place.pos, gather_blocks(mlp[0].astype(BF)), False)
        att_w1, = assemble("att", place.pos, gather_blocks(att[1].astype(BF)), False)
        mlp_w1, = assemble("mlp", place.pos, gather_blocks(mlp[1].astype(BF)), False)
    else:
        att_parts = mlp_parts = None

        def whole(w, axis):
            return lax.all_gather(w.astype(BF), "dp", axis=axis, tiled=True)

        full = [whole(w, 2) for w in (w_qkv, w_proj, w_fc1)] + [whole(w_fc2, 1)]
        gains_all, biases_all = whole(norm_gains, 2), whole(biases, 1)
        att_w0, att_w1 = (jnp.concatenate([full[0][l].T, full[1][l].T]) for l in range(LAYERS))
        mlp_w0, mlp_w1 = (jnp.concatenate([full[2][l].T, full[3][l]]) for l in range(LAYERS))
        vec0, vec1 = (whole_small(gains_all[l], biases_all[l]) for l in range(LAYERS))

    h0, a0, qkv0 = k.qkv_first(x, vec0, att_w0)
    o0, lse0 = k.attend(qkv0)
    mid0, b0, act0, slope0, h1 = k.mlp(h0, o0, vec0, att_w0, mlp_w0)
    a1, qkv1 = k.qkv(h1, vec1, att_w1)
    o1, lse1 = k.attend(qkv1)
    mid1, b1, act1, slope1, h2 = k.mlp(h1, o1, vec1, att_w1, mlp_w1)
    layer_out, g = k.finish(h2, cot)
    dm, du, g1, dp, do, small1a = k.mlp_back(g, mid1, slope1, vec1, att_w1, mlp_w1)
    mlp1 = k.outer("outer_mlp1", [(du, b1), (act1, dm)], mlp_parts)
    dqkv = k.attend_back(qkv1, do, lse1)
    att1 = k.outer("outer_att1", [(dqkv, a1), (dp, o1)], att_parts)
    g, small1b = k.qkv_back(h1, g1, dqkv, vec1, att_w1)
    dm, du, g1, dp, do, small0a = k.mlp_back(g, mid0, slope0, vec0, att_w0, mlp_w0)
    mlp0 = k.outer("outer_mlp0", [(du, b0), (act0, dm)], mlp_parts)
    dqkv = k.attend_back(qkv0, do, lse0)
    g, small0b = k.qkv_back(h0, g1, dqkv, vec0, att_w0)
    smalls = (small0a, small0b, small1a, small1b)
    att0 = k.outer("outer_att0", [(dqkv, a0), (dp, o0)], att_parts, smalls if fast else ())
    input_grad = k.unpack(g)

    if fast:
        size = att[0].shape[0]
        mlp_g1 = in_order(place.core, *scatter_blocks(*mlp1))
        att_g1 = in_order(place.core, *scatter_blocks(*att1))
        mlp_g0 = in_order(place.core, *scatter_blocks(*mlp0))
        mine, other = scatter_blocks(*att0)
        att_g0 = in_order(place.core, mine[:size], other[:size])
        pair = in_order(place.core, mine[size : size + 2], other[size : size + 2]).reshape(LAYERS, 1, 2, D)
        squares = sum(jnp.sum(t * t) for t in (att_g0, mlp_g0, att_g1, mlp_g1))
        rows = lax.dynamic_update_slice(jnp.zeros((LAYERS, 8, 2, D), F32), pair, (0, dp_index, 0, 0))
        packed = jnp.concatenate([rows.reshape(-1, D), jnp.full((8, D), squares)])
        packed = sum_chips(packed)
        small_g = packed[: LAYERS * SMALL].reshape(LAYERS, SMALL, D)
        squares = packed[LAYERS * SMALL, 0] + jnp.sum(small_g * small_g)
        shards = [att_g0, att_g1, mlp_g0, mlp_g1]
        cut = w_qkv.shape[2]
        grads = [
            jnp.stack([att_g0[:cut].T, att_g1[:cut].T]),
            jnp.stack([att_g0[cut:].T, att_g1[cut:].T]),
            jnp.stack([mlp_g0[: w_fc1.shape[2]].T, mlp_g1[: w_fc1.shape[2]].T]),
            jnp.stack([mlp_g0[w_fc1.shape[2] :], mlp_g1[w_fc1.shape[2] :]]),
        ]
    else:
        small_g = lax.psum(jnp.stack([small0a + small0b, small1a + small1b]), ("dp", "tok"))

        def part(rows):
            return lax.psum(lax.psum_scatter(rows.astype(F32), "dp", scatter_dimension=0, tiled=True), "tok")

        grads = [
            jnp.stack([part(t[: 3 * D]).T for t in (att0, att1)]),
            jnp.stack([part(t[3 * D :]).T for t in (att0, att1)]),
            jnp.stack([part(t[:FF]).T for t in (mlp0, mlp1)]),
            jnp.stack([part(t[FF:]) for t in (mlp0, mlp1)]),
        ]
        squares = lax.psum(sum(jnp.sum(t * t) for t in grads), "dp") + jnp.sum(small_g * small_g)
    gains_g = small_g[:, GAIN1 : GAIN2 + 1]
    biases_g = small_g[:, :10].reshape(LAYERS, -1)
    grads.append(lax.dynamic_slice_in_dim(gains_g, dp_index * norm_gains.shape[2], norm_gains.shape[2], 2))
    grads.append(lax.dynamic_slice_in_dim(biases_g, dp_index * biases.shape[1], biases.shape[1], 1))
    grad_norm = jnp.sqrt(squares)
    limit = 0.25 * math.sqrt(LAYERS * (4 * D * D + 2 * D * FF + 8 * D + FF))
    factor = jnp.minimum(1.0, limit / (grad_norm + 1e-06))
    masters = (w_qkv, w_proj, w_fc1, w_fc2, norm_gains, biases)
    moments = (mom_qkv, mom_proj, mom_fc1, mom_fc2, mom_gains, mom_biases)
    states, seconds = [], []
    for index in range(6):
        rate, decay = (0.08, 0.05) if index < 4 else (0.4, 0.0)
        state, second = adamw(masters[index], moments[index], grads[index] * factor, rate, decay)
        states.append(state)
        seconds.append(second.reshape(-1))
    return (layer_out, input_grad, grad_norm, *states, jnp.concatenate(seconds))


def solution(mesh):
    rows = P(("dp", "tok"), None, None)
    weights = (P(None, None, "dp"),) * 3 + (P(None, "dp", None), P(None, None, "dp"), P(None, "dp"))
    stacked = tuple(P(None, *spec) for spec in weights)
    return jax.shard_map(
        on_device,
        mesh=mesh,
        in_specs=(rows, rows, P("dp"), *weights, *stacked),
        out_specs=(rows, rows, P(), *stacked, P("dp")),
        check_vma=False,
    )
```

```python
import functools
import math

import jax
import jax.numpy as jnp
from jax import lax
from jax.experimental import pallas as pl
from jax.experimental.pallas import tpu as pltpu
from jax.sharding import PartitionSpec as P

D = 384
HEADS = 6
HD = 64
FF = 1536
LAYERS = 2
STEP = 10
PAIRS = HEADS // 2
TILE = 128
BIG = 256
EPS = 1e-06
HALF_ROOT = 0.7071067811865476
INV_ROOT_TAU = 0.3989422804014327
LOG2E = 1.4426950408889634
SCORE = 0.125 * LOG2E
TAIL_P = 0.4
TAIL = (
    0.22480539044849576,
    0.2382192213985389,
    0.13072083829499273,
    0.43284363894582684,
    -0.41172890451981375,
    0.7191256145749827,
    -0.41194367033429247,
    0.07795786677173361,
)
BF = jnp.bfloat16
F32 = jnp.float32


def nn(a, b):
    return lax.dot_general(a, b, (((1,), (0,)), ((), ())), preferred_element_type=F32)


def nt(a, b):
    return lax.dot_general(a, b, (((1,), (1,)), ((), ())), preferred_element_type=F32)


def tn(a, b):
    return lax.dot_general(a, b, (((0,), (0,)), ((), ())), preferred_element_type=F32)


def normalize(hidden):
    centered = hidden - jnp.mean(hidden, -1, keepdims=True)
    variance = jnp.mean(centered * centered, -1, keepdims=True)
    inverse = lax.rsqrt(variance + EPS)
    return centered * inverse, inverse


def norm_back(grad_n, normed, inverse):
    first = jnp.mean(grad_n, -1, keepdims=True)
    second = jnp.mean(grad_n * normed, -1, keepdims=True)
    return inverse * (grad_n - first - normed * second)


def gelu_pair(u):
    t = 1.0 / (1.0 + (TAIL_P * HALF_ROOT) * jnp.abs(u))
    bell = jnp.exp2(u * u * (-0.5 * LOG2E))
    poly = jnp.full_like(t, 0.5 * TAIL[-1])
    for coef in TAIL[-2::-1]:
        poly = poly * t + 0.5 * coef
    low = poly * t * bell
    cdf = jnp.where(u < 0.0, low, 1.0 - low)
    return u * cdf, cdf + u * bell * INV_ROOT_TAU


def both_heads(x):
    lane = lax.broadcasted_iota(jnp.int32, x.shape, 1)
    zero = jnp.zeros_like(x)
    return jnp.concatenate([jnp.where(lane < HD, x, zero), jnp.where(lane >= HD, x, zero)], 0)


def pick(both):
    half = both.shape[0] // 2
    lane = lax.broadcasted_iota(jnp.int32, (half, 2 * HD), 1)
    return jnp.where(lane < HD, both[:half], both[half:])


QB = 128


def by_length(meta, seqs, slots, run):
    full = -(-slots // 16) * 16
    sizes = [(w, -(-w // QB)) for w in (64, 128, 160) if w < full] + [(full, -(-full // QB))]

    def body(i, carry):
        length, start = meta[i], pl.multiple_of(meta[seqs + i], 16)
        low = 0
        for keys, blocks in sizes:
            pl.when(jnp.logical_and(length > low, length <= keys))(
                functools.partial(run, i, start, length, keys, blocks)
            )
            low = keys
        return carry

    lax.fori_loop(0, seqs, body, 0)


def attend(meta, seqs, slots, qkv_ref, o_ref, lse_ref):
    def run(i, start, length, keys, blocks):
        rows = pl.ds(start, keys)
        keep = lax.broadcasted_iota(jnp.int32, (keys, 2 * QB), 0) < length
        for pair in range(PAIRS):
            at = pair * 2 * HD
            k = qkv_ref[rows, D + at : D + at + 2 * HD]
            v = qkv_ref[rows, 2 * D + at : 2 * D + at + 2 * HD]
            for block in range(blocks):
                part = pl.ds(start + block * QB, QB)
                q = both_heads(qkv_ref[part, at : at + 2 * HD])
                s = jnp.where(keep, nt(k, q), -1e30)
                top = jnp.max(s, 0, keepdims=True)
                e = jnp.exp2((s - top) * SCORE)
                total = jnp.sum(e, 0, keepdims=True)
                p = (e * (1.0 / total)).astype(BF)
                o_ref[part, at : at + 2 * HD] = pick(tn(p, v)).astype(BF)
                lse_ref[i, pair : pair + 1, block * 2 * QB : (block + 1) * 2 * QB] = top * SCORE + jnp.log2(total)

    by_length(meta, seqs, slots, run)


def attend_back(meta, seqs, slots, qkv_ref, do_ref, lse_ref, dqkv_ref):
    def run(i, start, length, keys, blocks):
        rows = pl.ds(start, keys)
        keep = lax.broadcasted_iota(jnp.int32, (keys, 2 * QB), 0) < length
        for pair in range(PAIRS):
            at = pair * 2 * HD
            k = qkv_ref[rows, D + at : D + at + 2 * HD]
            v = qkv_ref[rows, 2 * D + at : 2 * D + at + 2 * HD]
            dk, dv = 0.0, 0.0
            for block in range(blocks):
                part = pl.ds(start + block * QB, QB)
                q = both_heads(qkv_ref[part, at : at + 2 * HD])
                do = do_ref[part, at : at + 2 * HD]
                row = lax.broadcasted_iota(jnp.int32, do.shape, 0)
                do = both_heads(jnp.where(row < length - block * QB, do, jnp.zeros_like(do)))
                lse = lse_ref[i, pair : pair + 1, block * 2 * QB : (block + 1) * 2 * QB]
                p = jnp.where(keep, jnp.exp2(nt(k, q) * SCORE - lse), 0.0)
                dp = nt(v, do)
                inner = jnp.sum(p * dp, 0, keepdims=True)
                ds = (p * (dp - inner)).astype(BF)
                dv = dv + nn(p.astype(BF), do)
                dk = dk + nn(ds, q)
                dqkv_ref[part, at : at + 2 * HD] = (pick(tn(ds, k)) * 0.125).astype(BF)
            dqkv_ref[rows, D + at : D + at + 2 * HD] = (dk * 0.125).astype(BF)
            dqkv_ref[rows, 2 * D + at : 2 * D + at + 2 * HD] = dv.astype(BF)

    by_length(meta, seqs, slots, run)


def over_rows(tiles, body):
    def step(t, carry):
        body(pl.ds(pl.multiple_of(t * BIG, BIG), BIG))
        return carry

    lax.fori_loop(0, tiles // 2, step, 0)
    odd = tiles % 2 == 1
    pl.when(odd)(lambda: body(pl.ds(pl.multiple_of((tiles - 1) * TILE, TILE), TILE)))


def zero_tail(tiles, total, refs):
    def body(t, carry):
        rows = pl.ds(pl.multiple_of(t * TILE, TILE), TILE)
        for ref in refs:
            ref[rows, :] = jnp.zeros((TILE, ref.shape[1]), ref.dtype)
        return carry

    lax.fori_loop(tiles, total, body, 0)


B_LN1, B_Q, B_V, B_PROJ, B_LN2, B_2, B_1, GAIN1, GAIN2 = 0, 1, 2, 3, 4, 5, 6, 10, 11
SMALL = 16


def row(ref, index, count=1):
    return jnp.concatenate([ref[index + i : index + i + 1, :] for i in range(count)], 1)


def add_row(ref, index, value):
    total = jnp.sum(value, 0, keepdims=True)
    for i in range(value.shape[1] // D):
        ref[index + i : index + i + 1, :] += total[:, i * D : (i + 1) * D]


def phase_qkv(tiles, h_ref, vec, att_w, a_ref, qkv_ref):
    def body(rows):
        normed, _ = normalize(h_ref[rows, :])
        a = (normed * row(vec, GAIN1) + row(vec, B_LN1)).astype(BF)
        a_ref[rows, :] = a
        bias = jnp.concatenate([row(vec, B_Q), jnp.zeros((1, D), F32), row(vec, B_V)], 1)
        qkv_ref[rows, :] = (nt(a, att_w[0 : 3 * D, :]) + bias).astype(BF)

    over_rows(tiles, body)


def phase_mlp(tiles, h_ref, o_ref, vec, att_w, mlp_w, mid_ref, a_ref, act_ref, slope_ref, out_ref):
    wide = 2 * D

    def body(rows):
        mid = h_ref[rows, :] + nt(o_ref[rows, :], att_w[3 * D :, :]) + row(vec, B_PROJ)
        mid_ref[rows, :] = mid
        normed, _ = normalize(mid)
        a = (normed * row(vec, GAIN2) + row(vec, B_LN2)).astype(BF)
        a_ref[rows, :] = a
        for c in range(0, FF, wide):
            u = nt(a, mlp_w[c : c + wide, :]) + row(vec, B_1 + c // D, wide // D)
            act, slope = gelu_pair(u)
            act_ref[rows, c : c + wide] = act.astype(BF)
            slope_ref[rows, c : c + wide] = slope
        out_ref[rows, :] = mid + nn(act_ref[rows, :], mlp_w[FF:, :]) + row(vec, B_2)

    over_rows(tiles, body)


def phase_mlp_back(tiles, g_ref, mid_ref, slope_ref, vec, att_w, mlp_w, dm_ref, du_ref, g1_ref, dp_ref, do_ref, small):
    wide = 2 * D

    def body(rows):
        g = g_ref[rows, :]
        dm = g.astype(BF)
        dm_ref[rows, :] = dm
        add_row(small, B_2, dm.astype(F32))
        for c in range(0, FF, wide):
            du = (nt(dm, mlp_w[FF + c : FF + c + wide, :]) * slope_ref[rows, c : c + wide]).astype(BF)
            du_ref[rows, c : c + wide] = du
            add_row(small, B_1 + c // D, du.astype(F32))
        da = nn(du_ref[rows, :], mlp_w[0:FF, :])
        normed, inverse = normalize(mid_ref[rows, :])
        add_row(small, GAIN2, da * normed)
        add_row(small, B_LN2, da)
        g1 = g + norm_back(da * row(vec, GAIN2), normed, inverse)
        g1_ref[rows, :] = g1
        dp = g1.astype(BF)
        dp_ref[rows, :] = dp
        add_row(small, B_PROJ, dp.astype(F32))
        do_ref[rows, :] = nn(dp, att_w[3 * D :, :]).astype(BF)

    over_rows(tiles, body)


def phase_qkv_back(tiles, h_ref, g1_ref, dqkv_ref, vec, att_w, g_out, small):
    def body(rows):
        dqkv = dqkv_ref[rows, :]
        add_row(small, B_Q, dqkv[:, 0:D].astype(F32))
        add_row(small, B_V, dqkv[:, 2 * D :].astype(F32))
        da = nn(dqkv, att_w[0 : 3 * D, :])
        normed, inverse = normalize(h_ref[rows, :])
        add_row(small, GAIN1, da * normed)
        add_row(small, B_LN1, da)
        g_out[rows, :] = g1_ref[rows, :] + norm_back(da * row(vec, GAIN1), normed, inverse)

    over_rows(tiles, body)


def outer_products(tiles, total, jobs):
    wide, low = 3 * 128, 0
    for size in sorted(set(min(k, total) for k in (3, 4, 5, 6, total))):

        def run(size=size):
            rows = size * TILE
            for left, right, result in jobs:
                for m in range(0, left.shape[1], wide):
                    result[m : m + wide, :] = tn(left[0:rows, m : m + wide], right[0:rows, :]).astype(result.dtype)

        pl.when(jnp.logical_and(tiles > low, tiles <= size))(run)
        low = size


def on_chip(shape, dtype):
    return pltpu.VMEM(shape, dtype)


def anywhere(shape, dtype):
    return jax.ShapeDtypeStruct(shape, dtype)


def call(body, name, outs, scratch, us, *arrays):
    specs, placed = [], []
    for a in arrays:
        if a.dtype == jnp.int32:
            specs.append(pl.BlockSpec(memory_space=pltpu.SMEM))
            placed.append(a)
        else:
            specs.append(pl.BlockSpec(memory_space=pltpu.VMEM))
            placed.append(pltpu.with_memory_space_constraint(a, pltpu.VMEM) if a.ndim == 2 else a)
    return pl.pallas_call(
        body,
        name=name,
        out_shape=list(outs),
        in_specs=specs,
        out_specs=[pl.BlockSpec(memory_space=pltpu.VMEM)] * len(outs),
        scratch_shapes=list(scratch),
        compiler_params=pltpu.CompilerParams(vmem_limit_bytes=(24 if name == 'apply_adamw' else 16) << 20),
        cost_estimate=pl.CostEstimate(flops=int(us * 1e9), bytes_accessed=0, transcendentals=0),
    )(*placed)


def plan_rows(lengths):
    room = (lengths + 15) // 16 * 16
    ends = jnp.cumsum(room)
    tiles = (ends[-1:] + TILE - 1) // TILE
    return jnp.concatenate([lengths, ends - room, tiles]).astype(jnp.int32)


def packed_tiles(seqs, slots):
    full = -(-slots // 16) * 16
    return -(-(seqs * full) // TILE)


class Kernels:
    def __init__(self, meta, seqs, slots):
        self.meta, self.seqs, self.slots = meta, seqs, slots
        self.total = packed_tiles(seqs, slots)
        self.rows = self.total * TILE

    def wait(self, *others):
        self.meta = after(self.meta, *others)

    def wide(self, width, dtype):
        return on_chip((self.rows, width), dtype)

    def lse(self):
        return on_chip((self.seqs, 8, -(-self.slots // QB) * 2 * QB), F32)

    def tiles(self, meta):
        return meta[2 * self.seqs]

    def spans(self, meta):
        for i in range(self.seqs):
            start = pl.multiple_of(meta[self.seqs + i], 16)
            keep = lax.broadcasted_iota(jnp.int32, (self.slots, D), 0) < meta[i]
            yield i, pl.ds(start, self.slots), keep

    def qkv_first(self, x, vec, att_w):
        def body(meta, x_ref, vec, att_w, h, a, qkv):
            h[...] = jnp.zeros_like(h)
            for i, rows, _ in self.spans(meta):
                h[rows, :] = x_ref[i].astype(F32)
            phase_qkv(self.tiles(meta), h, vec, att_w, a, qkv)
            zero_tail(self.tiles(meta), self.total, [a, qkv])

        outs = [self.wide(D, F32), self.wide(D, BF), self.wide(3 * D, BF)]
        return call(body, "qkv_first", outs, [], 2.5, self.meta, x, vec, att_w)

    def qkv(self, h, vec, att_w):
        def body(meta, h, vec, att_w, a, qkv):
            phase_qkv(self.tiles(meta), h, vec, att_w, a, qkv)
            zero_tail(self.tiles(meta), self.total, [a, qkv])

        return call(body, "qkv", [self.wide(D, BF), self.wide(3 * D, BF)], [], 2, self.meta, h, vec, att_w)

    def attend(self, qkv):
        def body(meta, qkv, o, lse):
            o[...] = jnp.zeros_like(o)
            lse[...] = jnp.zeros_like(lse)
            attend(meta, self.seqs, self.slots, qkv, o, lse)

        return call(body, "attend", [self.wide(D, BF), self.lse()], [], 4, self.meta, qkv)

    def mlp(self, h, o, vec, att_w, mlp_w):
        def body(meta, h, o, vec, att_w, mlp_w, mid, a, act, slope, out):
            phase_mlp(self.tiles(meta), h, o, vec, att_w, mlp_w, mid, a, act, slope, out)
            zero_tail(self.tiles(meta), self.total, [a, act])

        outs = [self.wide(D, F32), self.wide(D, BF), self.wide(FF, BF), self.wide(FF, F32), self.wide(D, F32)]
        return call(body, "mlp", outs, [], 6, self.meta, h, o, vec, att_w, mlp_w)

    def finish(self, h, cot):
        def body(meta, h, cot, out, g):
            g[...] = jnp.zeros_like(g)
            for i, rows, keep in self.spans(meta):
                out[i] = jnp.where(keep, h[rows, :], 0.0).astype(BF)
                g[rows, :] = jnp.where(keep, cot[i].astype(F32), 0.0)

        return call(body, "finish", [anywhere(cot.shape, BF), self.wide(D, F32)], [], 1, self.meta, h, cot)

    def mlp_back(self, g, mid, slope, vec, att_w, mlp_w):
        def body(meta, g, mid, slope, vec, att_w, mlp_w, dm, du, g1, dp, do, small):
            small[...] = jnp.zeros_like(small)
            phase_mlp_back(self.tiles(meta), g, mid, slope, vec, att_w, mlp_w, dm, du, g1, dp, do, small)
            zero_tail(self.tiles(meta), self.total, [dm, du, dp, do])

        outs = [self.wide(D, BF), self.wide(FF, BF), self.wide(D, F32), self.wide(D, BF), self.wide(D, BF)]
        outs.append(on_chip((SMALL, D), F32))
        return call(body, "mlp_back", outs, [], 4, self.meta, g, mid, slope, vec, att_w, mlp_w)

    def attend_back(self, qkv, do, lse):
        def body(meta, qkv, do, lse, dqkv):
            dqkv[...] = jnp.zeros_like(dqkv)
            attend_back(meta, self.seqs, self.slots, qkv, do, lse, dqkv)

        return call(body, "attend_back", [self.wide(3 * D, BF)], [], 6, self.meta, qkv, do, lse)[0]

    def qkv_back(self, h, g1, dqkv, vec, att_w):
        def body(meta, h, g1, dqkv, vec, att_w, g, small):
            small[...] = jnp.zeros_like(small)
            phase_qkv_back(self.tiles(meta), h, g1, dqkv, vec, att_w, g, small)

        outs = [self.wide(D, F32), on_chip((SMALL, D), F32)]
        return call(body, "qkv_back", outs, [], 2, self.meta, h, g1, dqkv, vec, att_w)

    def unpack(self, g):
        def body(meta, g, out):
            for i, rows, keep in self.spans(meta):
                out[i] = jnp.where(keep, g[rows, :], 0.0)

        return call(body, "unpack", [anywhere((self.seqs, self.slots, D), F32)], [], 1, self.meta, g)[0]

    def outer(self, name, pairs, parts=None, smalls=()):
        height = sum(left.shape[1] for left, _ in pairs)
        count = len(pairs)

        def products(meta, refs, result):
            jobs, base = [], 0
            for i in range(count):
                left, right = refs[2 * i], refs[2 * i + 1]
                jobs.append((left, right, result.at[base : base + left.shape[1]]))
                base += left.shape[1]
            outer_products(self.tiles(meta), self.total, jobs)

        flat = [a for pair in pairs for a in pair]
        if parts is None:
            def body(meta, *refs):
                products(meta, refs, refs[-1])

            return call(body, name, [on_chip((height, D), BF)], [], 2, self.meta, *flat)[0]

        extra = 8 if smalls else 0
        size = height // 16

        def body(meta, pos, *refs):
            small_refs = refs[2 * count : 2 * count + len(smalls)]
            outs, result = refs[2 * count + len(smalls) : 2 * count + len(smalls) + 4], refs[-1 - (extra > 0)]
            products(meta, refs, result)
            if extra:
                held = refs[-1]
                held[...] = jnp.zeros_like(held)
                for layer in range(LAYERS):
                    own = small_refs[2 * layer][...] + small_refs[2 * layer + 1][...]
                    for d in range(8):
                        held[layer, d, 0:2, :] = own[2 * d : 2 * d + 2, :]
            for out, side, x_rel in zip(outs, (0, 0, 1, 1), (0, 1, 0, 1)):
                for z_rel in range(4):
                    shard, half, pieces = parts(pos, side, x_rel, z_rel)
                    for at, source, n in pieces:
                        out[z_rel, at : at + n, :] = result[pl.ds(source, n), :]
                    if extra:
                        out[z_rel, size : size + extra, :] = held[half, shard].astype(BF)

        outs = [anywhere((4, size + extra, D), BF)] * 4
        scratch = [on_chip((height, D), BF)] + ([on_chip((LAYERS, 8, 8, D), F32)] if extra else [])
        return call(body, name, outs, scratch, 3, self.meta, parts.pos, *flat, *smalls)


def swap(x, axis, bit):
    return lax.ppermute(x, axis, [(i, i ^ bit) for i in range(lax.axis_size(axis))])


def fast_mesh():
    return lax.axis_size("dp") == 8 and lax.axis_size("tok") == 4


class Place:
    def __init__(self):
        dp, tok = lax.axis_index("dp"), lax.axis_index("tok")
        self.z, self.x, self.core = dp // 2, dp % 2, tok % 2
        self.pos = jnp.stack([self.z, self.x, self.core]).astype(jnp.int32)


def block_rows(kind, pos, side, x_rel, z_rel):
    shard = (pos[0] ^ z_rel) * 2 + (pos[1] ^ x_rel)
    half = pos[2] ^ side
    if kind == "mlp":
        return shard, half, [(0, pl.multiple_of(half * FF + shard * (FF // 8), 16), FF // 8)]
    n = D // 8
    pieces = []
    for s in range(2):
        u = half * 2 + s
        source = jnp.where(u < 3, shard * 3 * n + u * n, 3 * D + shard * n)
        pieces.append((s * n, pl.multiple_of(source, 16), n))
    return shard, half, pieces


class Parts:
    def __init__(self, kind, pos):
        self.kind, self.pos = kind, pos

    def __call__(self, pos, side, x_rel, z_rel):
        return block_rows(self.kind, pos, side, x_rel, z_rel)


def assemble(kind, pos, blocks, with_small):
    size = 2 * D // 16 * 2 if kind == "att" else FF // 8
    height = 4 * D if kind == "att" else 2 * FF

    def body(pos, *refs):
        blocks, out = refs[:4], refs[4]
        for block, side, x_rel in zip(blocks, (0, 0, 1, 1), (0, 1, 0, 1)):
            for z_rel in range(4):
                _, _, pieces = block_rows(kind, pos, side, x_rel, z_rel)
                for at, target, n in pieces:
                    out[pl.ds(target, n), :] = block[z_rel, at : at + n, :]
        if with_small:
            for vec in refs[5:]:
                vec[...] = jnp.zeros_like(vec)
            for shard in range(8):
                z_rel = pos[0] ^ (shard // 2)
                near = blocks[0][z_rel, size : size + 8, :].astype(F32)
                far = blocks[1][z_rel, size : size + 8, :].astype(F32)
                rows = jnp.where(pos[1] == shard % 2, near, far)
                first = shard * 10 // 8
                for layer in range(LAYERS):
                    vec, base = refs[5 + layer], 4 * layer
                    vec[first : first + 2, :] += rows[base : base + 2, :]
                    vec[GAIN1 : GAIN1 + 2, :] += rows[base + 2 : base + 4, :]

    outs = [on_chip((height, D), BF)] + [on_chip((SMALL, D), F32)] * (LAYERS if with_small else 0)
    return call(body, "assemble_" + kind, outs, [], 1, pos, *blocks)


def spread_small(gains, biases, shard):
    out = []
    for layer in range(LAYERS):
        bias = lax.dynamic_update_slice(jnp.zeros((2 * D,), F32), biases[layer], (shard * (10 * D // 8) % D,))
        gain = lax.dynamic_update_slice(jnp.zeros((2, D), F32), gains[layer], (0, shard * (D // 8)))
        out += [bias.reshape(2, D), gain]
    return jnp.concatenate(out)


def after(x, *others):
    return lax.optimization_barrier((x, others))[0]


class Gather:
    def __init__(self, piece):
        self.piece = piece

    def along_z(self, *wait):
        piece = after(self.piece, *wait) if wait else self.piece
        self.near = jnp.stack([piece] + [swap(piece, "dp", 2 * k) for k in (1, 2, 3)])
        return self.near

    def along_x(self, *wait):
        near = after(self.near, *wait) if wait else self.near
        self.far = swap(near, "dp", 1)
        self.near_other = swap(near, "tok", 1)
        return self.far

    def blocks(self):
        return self.near, self.far, self.near_other, swap(self.far, "tok", 1)


class Scatter:
    def __init__(self, blocks):
        self.keep_near, self.keep_far, self.send_near, self.send_far = blocks

    def cores(self, *wait):
        self.away = (self.keep_far.astype(F32) + swap(self.send_far, "tok", 1).astype(F32)).astype(BF)
        self.near = self.keep_near.astype(F32) + swap(self.send_near, "tok", 1).astype(F32)
        return self.away

    def along_x(self, *wait):
        away = after(self.away, *wait) if wait else self.away
        self.near = self.near + swap(away, "dp", 1).astype(F32)
        self.low = self.near[1:].astype(BF)
        return self.low

    def along_z(self, *wait):
        low = after(self.low, *wait) if wait else self.low
        got = [swap(low[i - 1], "dp", 2 * i) for i in (1, 2, 3)]
        self.mine = (self.near[0] + sum(t.astype(F32) for t in got)).astype(BF)
        return self.mine

    def along_y(self, *wait):
        mine = after(self.mine, *wait) if wait else self.mine
        mine = (mine.astype(F32) + swap(mine, "tok", 2).astype(F32)).astype(BF)
        return mine, swap(mine, "tok", 1)


def in_order(core, mine, other):
    return jnp.where(core == 0, jnp.concatenate([mine, other]), jnp.concatenate([other, mine])).astype(F32)


def sum_chips(x):
    x = (x + swap(x, "dp", 2)) + (swap(x, "dp", 4) + swap(x, "dp", 6))
    return x + swap(x, "dp", 1)


def adamw(weight, moments, clipped, rate, decay):
    first_mom = 0.9 * moments[0] + 0.1 * clipped
    second_mom = 0.999 * moments[1] + 0.001 * clipped * clipped
    fixed_first = first_mom / (1.0 - 0.9**STEP)
    fixed_second = second_mom / (1.0 - 0.999**STEP)
    new_weight = weight - rate * (fixed_first / (jnp.sqrt(fixed_second) + 1e-08) + decay * weight)
    return (jnp.stack([new_weight, first_mom]), second_mom)


FLAT = 128


def flatten_rows(ref, n, wide, out, base):
    period = math.lcm(wide, FLAT) // wide
    lines = period * wide // FLAT
    lane = lax.broadcasted_iota(jnp.int32, (n // period, FLAT), 1)
    for r in range(lines):
        value = jnp.zeros((n // period, FLAT), F32)
        for j in range(period):
            low, high = max(FLAT * r, wide * j), min(FLAT * (r + 1), wide * (j + 1))
            while low < high:
                column, at = low - wide * j, low - FLAT * r
                stop = min(high, low + FLAT - column % FLAT)
                part = ref[column // FLAT, pl.ds(j, n // period, stride=period), :]
                shift = (at - column) % FLAT
                part = pltpu.roll(part, shift, 1) if shift else part
                value = jnp.where(jnp.logical_and(lane >= at, lane < at + stop - low), part, value)
                low = stop
        out[pl.ds(base + r, n // period, stride=lines), :] = value
    return base + n * wide // FLAT


def shard_grads(pos, att, mlp, shapes):
    (qc, pc, uc, dr) = shapes

    def body(pos, att_mine, att_other, mlp_mine, mlp_other, gq, gp, gu, gd, square, wide):
        size = (qc + pc) // 2
        first = pos[2] == 0
        low = jnp.where(first, att_mine[0:size, :], att_other[0:size, :]).astype(F32)
        high = jnp.where(first, att_other[0:size, :], att_mine[0:size, :]).astype(F32)
        wide[0:size, :] = low
        wide[size : 2 * size, :] = high
        up = jnp.where(first, mlp_mine[...], mlp_other[...]).astype(F32)
        down = jnp.where(first, mlp_other[...], mlp_mine[...]).astype(F32)
        total = jnp.sum(low * low, 0, keepdims=True) + jnp.sum(high * high, 0, keepdims=True)
        total = total + jnp.sum(up * up, 0, keepdims=True) + jnp.sum(down * down, 0, keepdims=True)
        square[...] = jnp.broadcast_to(total, square.shape)
        gq[...] = wide[0:qc, :].T
        gp[...] = wide[qc : qc + pc, :].T
        gu[...] = up.T
        gd[...] = down

    outs = [on_chip((D, qc), F32), on_chip((D, pc), F32), on_chip((D, uc), F32), on_chip((dr, D), F32), on_chip((8, D), F32)]
    return call(body, "shard_grads", outs, [on_chip((qc + pc, D), F32)], 1.5, pos, *att, *mlp)


def apply_adamw(square, grads, masters, moments, small_second):
    shapes = [m.shape for m in moments]
    lines = sum(math.prod(t.shape) for t in masters) // FLAT + small_second.shape[0]

    def body(*refs):
        square, small_second = refs[0], refs[1]
        g_refs = (refs[2:6], refs[6:10])
        w_refs, m_refs = refs[10:14], refs[14:18]
        s_refs, out, padded = refs[18:22], refs[22], refs[23]
        factor = clip_factor(jnp.sqrt(square[0:1, 0:1]))
        base = 0
        for index in range(4):
            for layer in range(LAYERS):
                c = g_refs[layer][index][...] * factor
                w = w_refs[index][layer]
                first = 0.9 * m_refs[index][0, layer] + 0.1 * c
                second = 0.999 * m_refs[index][1, layer] + 0.001 * c * c
                root = jnp.sqrt(second * (1.0 / (1.0 - 0.999**STEP))) + 1e-08
                step = first * (1.0 / (1.0 - 0.9**STEP)) / root + 0.05 * w
                s_refs[index][0, layer] = w - 0.08 * step
                s_refs[index][1, layer] = first
                rows, cols = c.shape
                for at in range(0, cols, FLAT):
                    stop = min(at + FLAT, cols)
                    padded[at // FLAT, 0:rows, 0 : stop - at] = second[:, at:stop]
                base = flatten_rows(padded, rows, cols, out, base)
        out[base : base + small_second.shape[0], :] = small_second[...]

    outs = [anywhere(s, F32) for s in shapes] + [anywhere((lines, FLAT), F32)]
    flat = [t for layer in grads for t in layer]
    return call(body, "apply_adamw", outs, [on_chip((D // FLAT, D, FLAT), F32)], 5, square, small_second, *flat, *masters, *moments)


def clip_factor(norm):
    limit = 0.25 * math.sqrt(LAYERS * (4 * D * D + 2 * D * FF + 8 * D + FF))
    return jnp.minimum(1.0, limit / (norm + 1e-06))


def whole_small(gains, biases):
    rows = jnp.concatenate([biases.reshape(10, D), gains]).astype(F32)
    return jnp.pad(rows, ((0, SMALL - 12), (0, 0)))


def on_device(x, cot, lengths, w_qkv, w_proj, w_fc1, w_fc2, norm_gains, biases,
              mom_qkv, mom_proj, mom_fc1, mom_fc2, mom_gains, mom_biases):
    fast = fast_mesh()
    seqs, slots = x.shape[0], x.shape[1]
    own = lax.dynamic_slice_in_dim(lengths, lax.axis_index("tok") * seqs, seqs, 0)
    k = Kernels(plan_rows(own), seqs, slots)
    dp_index = lax.axis_index("dp")
    if fast:
        place = Place()
        att_parts, mlp_parts = Parts("att", place.pos), Parts("mlp", place.pos)

        def half(rows):
            size = rows.shape[0] // 2
            return lax.dynamic_slice_in_dim(rows, place.core * size, size, 0)

        small = spread_small(norm_gains, biases, dp_index)
        att = [half(jnp.concatenate([w_qkv[l].T, w_proj[l].T])) for l in range(LAYERS)]
        mlp = [jnp.where(place.core == 0, w_fc1[l].T, w_fc2[l]) for l in range(LAYERS)]
        size = att[0].shape[0]
        ga0 = Gather(jnp.concatenate([att[0], small]).astype(BF))
        gm0, ga1, gm1 = Gather(mlp[0].astype(BF)), Gather(att[1].astype(BF)), Gather(mlp[1].astype(BF))
        ga0.along_z()
        gm0.along_z(ga0.near)
        ga0.along_x()
        att_w0, vec0, vec1 = assemble("att", place.pos, ga0.blocks(), True)
    else:
        att_parts = mlp_parts = None

        def whole(w, axis):
            return lax.all_gather(w.astype(BF), "dp", axis=axis, tiled=True)

        full = [whole(w, 2) for w in (w_qkv, w_proj, w_fc1)] + [whole(w_fc2, 1)]
        gains_all, biases_all = whole(norm_gains, 2), whole(biases, 1)
        att_w0, att_w1 = (jnp.concatenate([full[0][l].T, full[1][l].T]) for l in range(LAYERS))
        mlp_w0, mlp_w1 = (jnp.concatenate([full[2][l].T, full[3][l]]) for l in range(LAYERS))
        vec0, vec1 = (whole_small(gains_all[l], biases_all[l]) for l in range(LAYERS))

    h0, a0, qkv0 = k.qkv_first(x, vec0, att_w0)
    if fast:
        gm0.along_x(qkv0)
        ga1.along_z(gm0.near, qkv0)
    o0, lse0 = k.attend(qkv0)
    if fast:
        mlp_w0, = assemble("mlp", place.pos, gm0.blocks(), False)
        ga1.along_x(gm0.far)
        gm1.along_z(ga1.near, gm0.far)
    mid0, b0, act0, slope0, h1 = k.mlp(h0, o0, vec0, att_w0, mlp_w0)
    if fast:
        gm1.along_x(ga1.far, h1)
        att_w1, = assemble("att", place.pos, ga1.blocks(), False)
    a1, qkv1 = k.qkv(h1, vec1, att_w1)
    o1, lse1 = k.attend(qkv1)
    if fast:
        mlp_w1, = assemble("mlp", place.pos, gm1.blocks(), False)
    mid1, b1, act1, slope1, h2 = k.mlp(h1, o1, vec1, att_w1, mlp_w1)
    layer_out, g = k.finish(h2, cot)
    dm, du, g1, dp, do, small1a = k.mlp_back(g, mid1, slope1, vec1, att_w1, mlp_w1)
    mlp1 = k.outer("outer_mlp1", [(du, b1), (act1, dm)], mlp_parts)
    k.wait(mlp1)
    dqkv = k.attend_back(qkv1, do, lse1)
    if fast:
        sm1 = Scatter(mlp1)
        k.wait(sm1.cores(), dqkv)
    att1 = k.outer("outer_att1", [(dqkv, a1), (dp, o1)], att_parts)
    k.wait(att1)
    g, small1b = k.qkv_back(h1, g1, dqkv, vec1, att_w1)
    dm, du, g1, dp, do, small0a = k.mlp_back(g, mid0, slope0, vec0, att_w0, mlp_w0)
    if fast:
        sa1 = Scatter(att1)
        k.wait(sa1.cores(), sm1.along_x(), dm)
    mlp0 = k.outer("outer_mlp0", [(du, b0), (act0, dm)], mlp_parts)
    k.wait(mlp0)
    dqkv = k.attend_back(qkv0, do, lse0)
    if fast:
        sm0 = Scatter(mlp0)
        k.wait(sm0.cores(), sa1.along_x(sm1.low), sm1.along_z(), dqkv)
    g, small0b = k.qkv_back(h0, g1, dqkv, vec0, att_w0)
    smalls = (small0a, small0b, small1a, small1b)
    att0 = k.outer("outer_att0", [(dqkv, a0), (dp, o0)], att_parts, smalls if fast else ())
    k.wait(att0)
    input_grad = k.unpack(g)

    if fast:
        sa0 = Scatter(att0)
        shapes = (w_qkv.shape[2], w_proj.shape[2], w_fc1.shape[2], w_fc2.shape[1])
        sm0.along_x(sa1.low)
        sa0.cores()
        sa1.along_z(sm1.mine)
        g1 = shard_grads(place.pos, sa1.along_y(), sm1.along_y(), shapes)
        sa0.along_x(sm0.low)
        sm0.along_z(sa1.mine)
        sa0.along_z(sm0.mine)
        mine, other = sa0.along_y()
        g0 = shard_grads(place.pos, (mine, other), sm0.along_y(), shapes)
        pair = in_order(place.core, mine[size : size + 2], other[size : size + 2]).reshape(LAYERS, 1, 2, D)
        rows = lax.dynamic_update_slice(jnp.zeros((LAYERS, 8, 2, D), F32), pair, (0, dp_index, 0, 0))
        packed = sum_chips(jnp.concatenate([rows.reshape(-1, D), g0[4] + g1[4]]))
        small_g = packed[: LAYERS * SMALL].reshape(LAYERS, SMALL, D)
        squares = jnp.sum(packed[LAYERS * SMALL]) + jnp.sum(small_g * small_g)
    else:
        small_g = lax.psum(jnp.stack([small0a + small0b, small1a + small1b]), ("dp", "tok"))

        def part(rows):
            return lax.psum(lax.psum_scatter(rows.astype(F32), "dp", scatter_dimension=0, tiled=True), "tok")

        grads = [
            jnp.stack([part(t[: 3 * D]).T for t in (att0, att1)]),
            jnp.stack([part(t[3 * D :]).T for t in (att0, att1)]),
            jnp.stack([part(t[:FF]).T for t in (mlp0, mlp1)]),
            jnp.stack([part(t[FF:]) for t in (mlp0, mlp1)]),
        ]
        squares = lax.psum(sum(jnp.sum(t * t) for t in grads), "dp") + jnp.sum(small_g * small_g)
    gains_g = small_g[:, GAIN1 : GAIN2 + 1]
    biases_g = small_g[:, :10].reshape(LAYERS, -1)
    grad_norm = jnp.sqrt(squares)
    factor = clip_factor(grad_norm)
    small_grads = (
        lax.dynamic_slice_in_dim(gains_g, dp_index * norm_gains.shape[2], norm_gains.shape[2], 2),
        lax.dynamic_slice_in_dim(biases_g, dp_index * biases.shape[1], biases.shape[1], 1),
    )
    smalls = [
        adamw(w, m, t * factor, 0.4, 0.0)
        for w, m, t in zip((norm_gains, biases), (mom_gains, mom_biases), small_grads)
    ]
    small_second = jnp.concatenate([second.reshape(-1) for _, second in smalls])
    masters, moments = (w_qkv, w_proj, w_fc1, w_fc2), (mom_qkv, mom_proj, mom_fc1, mom_fc2)
    if fast:
        small_second = small_second.reshape(-1, FLAT)
        square = jnp.broadcast_to(squares, (8, FLAT))
        *states, seconds = apply_adamw(square, (g0[:4], g1[:4]), masters, moments, small_second)
        seconds = seconds.reshape(-1)
    else:
        pairs = [adamw(w, m, t * factor, 0.08, 0.05) for w, m, t in zip(masters, moments, grads)]
        states = [state for state, _ in pairs]
        seconds = jnp.concatenate([second.reshape(-1) for _, second in pairs] + [small_second])
    return (layer_out, input_grad, grad_norm, *states, smalls[0][0], smalls[1][0], seconds)


def solution(mesh):
    rows = P(("dp", "tok"), None, None)
    weights = (P(None, None, "dp"),) * 3 + (P(None, "dp", None), P(None, None, "dp"), P(None, "dp"))
    stacked = tuple(P(None, *spec) for spec in weights)
    return jax.shard_map(
        on_device,
        mesh=mesh,
        in_specs=(rows, rows, P("dp"), *weights, *stacked),
        out_specs=(rows, rows, P(), *stacked, P("dp")),
        check_vma=False,
    )
```

```python
import functools
import math

import jax
import jax.numpy as jnp
from jax import lax
from jax.experimental import pallas as pl
from jax.experimental.pallas import tpu as pltpu
from jax.sharding import PartitionSpec as P

D = 384
HEADS = 6
HD = 64
FF = 1536
LAYERS = 2
STEP = 10
PAIRS = HEADS // 2
TILE = 128
BIG = 256
COST = 4e8
EPS = 1e-06
HALF_ROOT = 0.7071067811865476
INV_ROOT_TAU = 0.3989422804014327
LOG2E = 1.4426950408889634
SCORE = 0.125 * LOG2E
TAIL_P = 0.4
TAIL = (
    0.22480539044849576,
    0.2382192213985389,
    0.13072083829499273,
    0.43284363894582684,
    -0.41172890451981375,
    0.7191256145749827,
    -0.41194367033429247,
    0.07795786677173361,
)
BF = jnp.bfloat16
F32 = jnp.float32


def nn(a, b):
    return lax.dot_general(a, b, (((1,), (0,)), ((), ())), preferred_element_type=F32)


def nt(a, b):
    return lax.dot_general(a, b, (((1,), (1,)), ((), ())), preferred_element_type=F32)


def tn(a, b):
    return lax.dot_general(a, b, (((0,), (0,)), ((), ())), preferred_element_type=F32)


def normalize(hidden):
    centered = hidden - jnp.mean(hidden, -1, keepdims=True)
    variance = jnp.mean(centered * centered, -1, keepdims=True)
    inverse = lax.rsqrt(variance + EPS)
    return centered * inverse, inverse


def norm_back(grad_n, normed, inverse):
    first = jnp.mean(grad_n, -1, keepdims=True)
    second = jnp.mean(grad_n * normed, -1, keepdims=True)
    return inverse * (grad_n - first - normed * second)


def gelu_pair(u):
    t = 1.0 / (1.0 + (TAIL_P * HALF_ROOT) * jnp.abs(u))
    bell = jnp.exp2(u * u * (-0.5 * LOG2E))
    poly = jnp.full_like(t, 0.5 * TAIL[-1])
    for coef in TAIL[-2::-1]:
        poly = poly * t + 0.5 * coef
    low = poly * t * bell
    cdf = jnp.where(u < 0.0, low, 1.0 - low)
    return u * cdf, cdf + u * bell * INV_ROOT_TAU


def both_heads(x):
    lane = lax.broadcasted_iota(jnp.int32, x.shape, 1)
    zero = jnp.zeros_like(x)
    return jnp.concatenate([jnp.where(lane < HD, x, zero), jnp.where(lane >= HD, x, zero)], 0)


def pick(both):
    half = both.shape[0] // 2
    lane = lax.broadcasted_iota(jnp.int32, (half, 2 * HD), 1)
    return jnp.where(lane < HD, both[:half], both[half:])


QB = 128


def by_length(meta, seqs, slots, run):
    full = -(-slots // 16) * 16
    sizes = [(w, -(-w // QB)) for w in (64, 128, 160) if w < full] + [(full, -(-full // QB))]

    def body(i, carry):
        length, start = meta[i], pl.multiple_of(meta[seqs + i], 16)
        low = 0
        for keys, blocks in sizes:
            pl.when(jnp.logical_and(length > low, length <= keys))(
                functools.partial(run, i, start, length, keys, blocks)
            )
            low = keys
        return carry

    lax.fori_loop(0, seqs, body, 0)


def attend(meta, seqs, slots, qkv_ref, o_ref, lse_ref):
    def run(i, start, length, keys, blocks):
        rows = pl.ds(start, keys)
        keep = lax.broadcasted_iota(jnp.int32, (keys, 2 * QB), 0) < length
        for pair in range(PAIRS):
            at = pair * 2 * HD
            k = qkv_ref[rows, D + at : D + at + 2 * HD]
            v = qkv_ref[rows, 2 * D + at : 2 * D + at + 2 * HD]
            for block in range(blocks):
                part = pl.ds(start + block * QB, QB)
                q = both_heads(qkv_ref[part, at : at + 2 * HD])
                s = jnp.where(keep, nt(k, q), -1e30)
                top = jnp.max(s, 0, keepdims=True)
                e = jnp.exp2((s - top) * SCORE)
                total = jnp.sum(e, 0, keepdims=True)
                p = (e * (1.0 / total)).astype(BF)
                o_ref[part, at : at + 2 * HD] = pick(tn(p, v)).astype(BF)
                lse_ref[i, pair : pair + 1, block * 2 * QB : (block + 1) * 2 * QB] = top * SCORE + jnp.log2(total)

    by_length(meta, seqs, slots, run)


def attend_back(meta, seqs, slots, qkv_ref, do_ref, lse_ref, dqkv_ref):
    def run(i, start, length, keys, blocks):
        rows = pl.ds(start, keys)
        keep = lax.broadcasted_iota(jnp.int32, (keys, 2 * QB), 0) < length
        for pair in range(PAIRS):
            at = pair * 2 * HD
            k = qkv_ref[rows, D + at : D + at + 2 * HD]
            v = qkv_ref[rows, 2 * D + at : 2 * D + at + 2 * HD]
            dk, dv = 0.0, 0.0
            for block in range(blocks):
                part = pl.ds(start + block * QB, QB)
                q = both_heads(qkv_ref[part, at : at + 2 * HD])
                do = do_ref[part, at : at + 2 * HD]
                row = lax.broadcasted_iota(jnp.int32, do.shape, 0)
                do = both_heads(jnp.where(row < length - block * QB, do, jnp.zeros_like(do)))
                lse = lse_ref[i, pair : pair + 1, block * 2 * QB : (block + 1) * 2 * QB]
                p = jnp.where(keep, jnp.exp2(nt(k, q) * SCORE - lse), 0.0)
                dp = nt(v, do)
                inner = jnp.sum(p * dp, 0, keepdims=True)
                ds = (p * (dp - inner)).astype(BF)
                dv = dv + nn(p.astype(BF), do)
                dk = dk + nn(ds, q)
                dqkv_ref[part, at : at + 2 * HD] = (pick(tn(ds, k)) * 0.125).astype(BF)
            dqkv_ref[rows, D + at : D + at + 2 * HD] = (dk * 0.125).astype(BF)
            dqkv_ref[rows, 2 * D + at : 2 * D + at + 2 * HD] = dv.astype(BF)

    by_length(meta, seqs, slots, run)


def over_rows(tiles, body):
    def step(t, carry):
        body(pl.ds(pl.multiple_of(t * BIG, BIG), BIG))
        return carry

    lax.fori_loop(0, tiles // 2, step, 0)
    odd = tiles % 2 == 1
    pl.when(odd)(lambda: body(pl.ds(pl.multiple_of((tiles - 1) * TILE, TILE), TILE)))


def zero_tail(tiles, total, refs):
    def body(t, carry):
        rows = pl.ds(pl.multiple_of(t * TILE, TILE), TILE)
        for ref in refs:
            ref[rows, :] = jnp.zeros((TILE, ref.shape[1]), ref.dtype)
        return carry

    lax.fori_loop(tiles, total, body, 0)


B_LN1, B_Q, B_V, B_PROJ, B_LN2, B_2, B_1, GAIN1, GAIN2 = 0, 1, 2, 3, 4, 5, 6, 10, 11
SMALL = 16


def row(ref, index, count=1):
    return jnp.concatenate([ref[index + i : index + i + 1, :] for i in range(count)], 1)


def add_row(ref, index, value):
    total = jnp.sum(value, 0, keepdims=True)
    for i in range(value.shape[1] // D):
        ref[index + i : index + i + 1, :] += total[:, i * D : (i + 1) * D]


def phase_qkv(tiles, h_ref, vec, att_w, a_ref, qkv_ref):
    def body(rows):
        normed, _ = normalize(h_ref[rows, :])
        a = (normed * row(vec, GAIN1) + row(vec, B_LN1)).astype(BF)
        a_ref[rows, :] = a
        bias = jnp.concatenate([row(vec, B_Q), jnp.zeros((1, D), F32), row(vec, B_V)], 1)
        qkv_ref[rows, :] = (nt(a, att_w[0 : 3 * D, :]) + bias).astype(BF)

    over_rows(tiles, body)


def phase_mlp(tiles, h_ref, o_ref, vec, att_w, mlp_w, mid_ref, a_ref, act_ref, slope_ref, out_ref):
    wide = 2 * D

    def body(rows):
        mid = h_ref[rows, :] + nt(o_ref[rows, :], att_w[3 * D :, :]) + row(vec, B_PROJ)
        mid_ref[rows, :] = mid
        normed, _ = normalize(mid)
        a = (normed * row(vec, GAIN2) + row(vec, B_LN2)).astype(BF)
        a_ref[rows, :] = a
        for c in range(0, FF, wide):
            u = nt(a, mlp_w[c : c + wide, :]) + row(vec, B_1 + c // D, wide // D)
            act, slope = gelu_pair(u)
            act_ref[rows, c : c + wide] = act.astype(BF)
            slope_ref[rows, c : c + wide] = slope
        out_ref[rows, :] = mid + nn(act_ref[rows, :], mlp_w[FF:, :]) + row(vec, B_2)

    over_rows(tiles, body)


def phase_mlp_back(tiles, g_ref, mid_ref, slope_ref, vec, att_w, mlp_w, dm_ref, du_ref, g1_ref, dp_ref, do_ref, small):
    wide = 2 * D

    def body(rows):
        g = g_ref[rows, :]
        dm = g.astype(BF)
        dm_ref[rows, :] = dm
        add_row(small, B_2, dm.astype(F32))
        for c in range(0, FF, wide):
            du = (nt(dm, mlp_w[FF + c : FF + c + wide, :]) * slope_ref[rows, c : c + wide]).astype(BF)
            du_ref[rows, c : c + wide] = du
            add_row(small, B_1 + c // D, du.astype(F32))
        da = nn(du_ref[rows, :], mlp_w[0:FF, :])
        normed, inverse = normalize(mid_ref[rows, :])
        add_row(small, GAIN2, da * normed)
        add_row(small, B_LN2, da)
        g1 = g + norm_back(da * row(vec, GAIN2), normed, inverse)
        g1_ref[rows, :] = g1
        dp = g1.astype(BF)
        dp_ref[rows, :] = dp
        add_row(small, B_PROJ, dp.astype(F32))
        do_ref[rows, :] = nn(dp, att_w[3 * D :, :]).astype(BF)

    over_rows(tiles, body)


def phase_qkv_back(tiles, h_ref, g1_ref, dqkv_ref, vec, att_w, g_out, small):
    def body(rows):
        dqkv = dqkv_ref[rows, :]
        add_row(small, B_Q, dqkv[:, 0:D].astype(F32))
        add_row(small, B_V, dqkv[:, 2 * D :].astype(F32))
        da = nn(dqkv, att_w[0 : 3 * D, :])
        normed, inverse = normalize(h_ref[rows, :])
        add_row(small, GAIN1, da * normed)
        add_row(small, B_LN1, da)
        g_out[rows, :] = g1_ref[rows, :] + norm_back(da * row(vec, GAIN1), normed, inverse)

    over_rows(tiles, body)


def outer_products(tiles, total, jobs):
    low = 0
    for size in sorted(set(min(k, total) for k in (4, 6, total))):

        def run(size=size):
            rows = size * TILE
            for left, right, result in jobs:
                wide = 2 * D if left.shape[1] % (2 * D) == 0 else D

                def step(m, carry, left=left, right=right, result=result, wide=wide):
                    at = pl.ds(pl.multiple_of(m * wide, 128), wide)
                    result[at, :] = tn(left[0:rows, at], right[0:rows, :]).astype(result.dtype)
                    return carry

                lax.fori_loop(0, left.shape[1] // wide, step, 0)

        pl.when(jnp.logical_and(tiles > low, tiles <= size))(run)
        low = size


def on_chip(shape, dtype):
    return pltpu.VMEM(shape, dtype)


def anywhere(shape, dtype):
    return jax.ShapeDtypeStruct(shape, dtype)


def call(body, name, outs, scratch, us, *arrays):
    specs, placed = [], []
    for a in arrays:
        if a.dtype == jnp.int32:
            specs.append(pl.BlockSpec(memory_space=pltpu.SMEM))
            placed.append(a)
        else:
            specs.append(pl.BlockSpec(memory_space=pltpu.VMEM))
            placed.append(pltpu.with_memory_space_constraint(a, pltpu.VMEM) if a.ndim == 2 else a)
    return pl.pallas_call(
        body,
        name=name,
        out_shape=list(outs),
        in_specs=specs,
        out_specs=[pl.BlockSpec(memory_space=pltpu.VMEM)] * len(outs),
        scratch_shapes=list(scratch),
        compiler_params=pltpu.CompilerParams(vmem_limit_bytes=16 << 20),
        cost_estimate=pl.CostEstimate(flops=int(us * COST), bytes_accessed=0, transcendentals=0),
    )(*placed)


def plan_rows(lengths):
    room = (lengths + 15) // 16 * 16
    ends = jnp.cumsum(room)
    tiles = (ends[-1:] + TILE - 1) // TILE
    return jnp.concatenate([lengths, ends - room, tiles]).astype(jnp.int32)


def packed_tiles(seqs, slots):
    full = -(-slots // 16) * 16
    return -(-(seqs * full) // TILE)


class Kernels:
    def __init__(self, meta, seqs, slots):
        self.meta, self.seqs, self.slots = meta, seqs, slots
        self.total = packed_tiles(seqs, slots)
        self.rows = self.total * TILE

    def wait(self, *others):
        self.meta = after(self.meta, *others)

    def wide(self, width, dtype):
        return on_chip((self.rows, width), dtype)

    def lse(self):
        return on_chip((self.seqs, 8, -(-self.slots // QB) * 2 * QB), F32)

    def tiles(self, meta):
        return meta[2 * self.seqs]

    def spans(self, meta):
        for i in range(self.seqs):
            start = pl.multiple_of(meta[self.seqs + i], 16)
            keep = lax.broadcasted_iota(jnp.int32, (self.slots, D), 0) < meta[i]
            yield i, pl.ds(start, self.slots), keep

    def qkv_first(self, x, vec, att_w):
        def body(meta, x_ref, vec, att_w, h, a, qkv):
            h[...] = jnp.zeros_like(h)
            for i, rows, _ in self.spans(meta):
                h[rows, :] = x_ref[i].astype(F32)
            phase_qkv(self.tiles(meta), h, vec, att_w, a, qkv)
            zero_tail(self.tiles(meta), self.total, [a, qkv])

        outs = [self.wide(D, F32), self.wide(D, BF), self.wide(3 * D, BF)]
        return call(body, "qkv_first", outs, [], 2.5, self.meta, x, vec, att_w)

    def attend(self, qkv):
        def body(meta, qkv, o, lse):
            o[...] = jnp.zeros_like(o)
            lse[...] = jnp.zeros_like(lse)
            attend(meta, self.seqs, self.slots, qkv, o, lse)

        return call(body, "attend", [self.wide(D, BF), self.lse()], [], 4, self.meta, qkv)

    def mlp(self, h, o, vec, att_w, mlp_w):
        def body(meta, h, o, vec, att_w, mlp_w, mid, a, act, slope, out):
            phase_mlp(self.tiles(meta), h, o, vec, att_w, mlp_w, mid, a, act, slope, out)
            zero_tail(self.tiles(meta), self.total, [a, act])

        outs = [self.wide(D, F32), self.wide(D, BF), self.wide(FF, BF), self.wide(FF, F32), self.wide(D, F32)]
        return call(body, "mlp", outs, [], 6, self.meta, h, o, vec, att_w, mlp_w)

    def qkv_attend(self, h, vec, att_w):
        def body(meta, h, vec, att_w, a, qkv, o, lse):
            phase_qkv(self.tiles(meta), h, vec, att_w, a, qkv)
            zero_tail(self.tiles(meta), self.total, [a, qkv])
            o[...] = jnp.zeros_like(o)
            lse[...] = jnp.zeros_like(lse)
            attend(meta, self.seqs, self.slots, qkv, o, lse)

        outs = [self.wide(D, BF), self.wide(3 * D, BF), self.wide(D, BF), self.lse()]
        return call(body, "qkv_attend", outs, [], 6, self.meta, h, vec, att_w)

    def pack(self, cot):
        def body(meta, cot, g):
            g[...] = jnp.zeros_like(g)
            for i, rows, keep in self.spans(meta):
                g[rows, :] = jnp.where(keep, cot[i].astype(F32), 0.0)

        return call(body, "pack", [self.wide(D, F32)], [], 1, self.meta, cot)[0]

    def mlp_back(self, name, g, mid, slope, vec, att_w, mlp_w, a, act, parts):
        results, held = self.blocks(2 * FF, parts, 0)

        def body(meta, pos, g, mid, slope, vec, att_w, mlp_w, a, act, g1, dp, do, small, *rest):
            outs, (dm, du) = rest[: len(results)], rest[len(results) : len(results) + 2]
            whole = rest[-1] if parts else outs[0]
            small[...] = jnp.zeros_like(small)
            phase_mlp_back(self.tiles(meta), g, mid, slope, vec, att_w, mlp_w, dm, du, g1, dp, do, small)
            zero_tail(self.tiles(meta), self.total, [dm, du, dp, do])
            outer_products(self.tiles(meta), self.total, [(du, a, whole.at[0:FF]), (act, dm, whole.at[FF : 2 * FF])])
            self.deal(pos, whole, outs, parts, None)

        outs = [self.wide(D, F32), self.wide(D, BF), self.wide(D, BF), on_chip((SMALL, D), F32)]
        scratch = [self.wide(D, BF), self.wide(FF, BF), *held]
        pos = parts.pos if parts else jnp.zeros((3,), jnp.int32)
        got = call(body, name, outs + results, scratch, 7, self.meta, pos, g, mid, slope, vec, att_w, mlp_w, a, act)
        return got[:4], got[4:]

    def attention_back(self, name, qkv, do, lse, h, g1, vec, att_w, a, dp, o, parts, smalls=()):
        extra = 8 if smalls else 0
        results, held = self.blocks(4 * D, parts, extra)

        def body(meta, pos, qkv, do, lse, h, g1, vec, att_w, a, dp, o, *rest):
            given, rest = rest[: len(smalls)], rest[len(smalls) :]
            g, small, outs = rest[0], rest[1], rest[2 : 2 + len(results)]
            dqkv = rest[2 + len(results)]
            whole = rest[3 + len(results)] if parts else outs[0]
            dqkv[...] = jnp.zeros_like(dqkv)
            small[...] = jnp.zeros_like(small)
            attend_back(meta, self.seqs, self.slots, qkv, do, lse, dqkv)
            phase_qkv_back(self.tiles(meta), h, g1, dqkv, vec, att_w, g, small)
            jobs = [(dqkv, a, whole.at[0 : 3 * D]), (dp, o, whole.at[3 * D : 4 * D])]
            outer_products(self.tiles(meta), self.total, jobs)
            rows = None
            if extra:
                rows = rest[-1]
                rows[...] = jnp.zeros_like(rows)
                for layer, own in enumerate((given[0][...] + small[...], given[1][...] + given[2][...])):
                    for d in range(8):
                        rows[layer, d, 0:2, :] = own[2 * d : 2 * d + 2, :]
            self.deal(pos, whole, outs, parts, rows)

        outs = [self.wide(D, F32), on_chip((SMALL, D), F32)]
        pos = parts.pos if parts else jnp.zeros((3,), jnp.int32)
        arrays = (qkv, do, lse, h, g1, vec, att_w, a, dp, o, *smalls)
        got = call(body, name, outs + results, [self.wide(3 * D, BF), *held], 9, self.meta, pos, *arrays)
        return got[:2], got[2:]

    def blocks(self, height, parts, extra):
        if parts is None:
            return [on_chip((height, D), BF)], []
        held = [on_chip((height, D), BF)] + ([on_chip((LAYERS, 8, 8, D), F32)] if extra else [])
        return [anywhere((4, height // 16 + extra, D), BF)] * 4, held

    def deal(self, pos, whole, outs, parts, rows):
        if parts is None:
            return
        size = whole.shape[0] // 16
        for out, side, x_rel in zip(outs, (0, 0, 1, 1), (0, 1, 0, 1)):
            for z_rel in range(4):
                shard, half, pieces = parts(pos, side, x_rel, z_rel)
                for at, source, n in pieces:
                    out[z_rel, at : at + n, :] = whole[pl.ds(source, n), :]
                if rows is not None:
                    out[z_rel, size : size + 8, :] = rows[half, shard].astype(BF)

    def unpack(self, name, g, dtype):
        def body(meta, g, out):
            for i, rows, keep in self.spans(meta):
                out[i] = jnp.where(keep, g[rows, :], 0.0).astype(dtype)

        return call(body, name, [anywhere((self.seqs, self.slots, D), dtype)], [], 1, self.meta, g)[0]


def swap(x, axis, bit):
    return lax.ppermute(x, axis, [(i, i ^ bit) for i in range(lax.axis_size(axis))])


def fast_mesh():
    return lax.axis_size("dp") == 8 and lax.axis_size("tok") == 4


class Place:
    def __init__(self):
        dp, tok = lax.axis_index("dp"), lax.axis_index("tok")
        self.z, self.x, self.core = dp // 2, dp % 2, tok % 2
        self.pos = jnp.stack([self.z, self.x, self.core]).astype(jnp.int32)


def block_rows(kind, pos, side, x_rel, z_rel):
    shard = (pos[0] ^ z_rel) * 2 + (pos[1] ^ x_rel)
    half = pos[2] ^ side
    if kind == "mlp":
        return shard, half, [(0, pl.multiple_of(half * FF + shard * (FF // 8), 16), FF // 8)]
    n = D // 8
    pieces = []
    for s in range(2):
        u = half * 2 + s
        source = jnp.where(u < 3, shard * 3 * n + u * n, 3 * D + shard * n)
        pieces.append((s * n, pl.multiple_of(source, 16), n))
    return shard, half, pieces


class Parts:
    def __init__(self, kind, pos):
        self.kind, self.pos = kind, pos

    def __call__(self, pos, side, x_rel, z_rel):
        return block_rows(self.kind, pos, side, x_rel, z_rel)


def assemble(kind, pos, blocks, with_small):
    size = 2 * D // 16 * 2 if kind == "att" else FF // 8
    height = 4 * D if kind == "att" else 2 * FF

    def body(pos, *refs):
        blocks, out = refs[:4], refs[4]
        for block, side, x_rel in zip(blocks, (0, 0, 1, 1), (0, 1, 0, 1)):
            for z_rel in range(4):
                _, _, pieces = block_rows(kind, pos, side, x_rel, z_rel)
                for at, target, n in pieces:
                    out[pl.ds(target, n), :] = block[z_rel, at : at + n, :]
        if with_small:
            for vec in refs[5:]:
                vec[...] = jnp.zeros_like(vec)
            for shard in range(8):
                z_rel = pos[0] ^ (shard // 2)
                near = blocks[0][z_rel, size : size + 8, :].astype(F32)
                far = blocks[1][z_rel, size : size + 8, :].astype(F32)
                rows = jnp.where(pos[1] == shard % 2, near, far)
                first = shard * 10 // 8
                for layer in range(LAYERS):
                    vec, base = refs[5 + layer], 4 * layer
                    vec[first : first + 2, :] += rows[base : base + 2, :]
                    vec[GAIN1 : GAIN1 + 2, :] += rows[base + 2 : base + 4, :]

    outs = [on_chip((height, D), BF)] + [on_chip((SMALL, D), F32)] * (LAYERS if with_small else 0)
    return call(body, "assemble_" + kind, outs, [], 1, pos, *blocks)


def spread_small(gains, biases, shard):
    out = []
    for layer in range(LAYERS):
        bias = lax.dynamic_update_slice(jnp.zeros((2 * D,), F32), biases[layer], (shard * (10 * D // 8) % D,))
        gain = lax.dynamic_update_slice(jnp.zeros((2, D), F32), gains[layer], (0, shard * (D // 8)))
        out += [bias.reshape(2, D), gain]
    return jnp.concatenate(out)


def after(x, *others):
    return lax.optimization_barrier((x, others))[0]


def hop(x, axis, bit, begin=(), end=()):
    got = swap(after(x, *begin) if begin else x, axis, bit)
    return after(got, *end) if end else got


class Gather:
    def __init__(self, piece):
        self.piece = piece

    def along_z(self, begin=(), end=()):
        self.near = jnp.stack([self.piece] + [hop(self.piece, "dp", 2 * k, begin, end) for k in (1, 2, 3)])

    def far_z(self, begin=(), end=()):
        self.pair = jnp.stack([self.piece, hop(self.piece, "dp", 4, begin, end)])

    def near_z(self, begin=(), end=()):
        got = hop(self.pair, "dp", 2, begin, end)
        self.near = jnp.stack([self.pair[0], got[0], self.pair[1], got[1]])

    def along_x(self, begin=(), end=()):
        self.far = hop(self.near, "dp", 1, begin, end)
        self.near_other = hop(self.near, "tok", 1, begin, end)

    def cores(self):
        self.far_other = swap(self.far, "tok", 1)
        return self.near, self.far, self.near_other, self.far_other


class Scatter:
    def __init__(self, blocks):
        self.keep_near, self.keep_far, self.send_near, self.send_far = blocks

    def cores(self, end=()):
        self.away = (self.keep_far.astype(F32) + swap(self.send_far, "tok", 1).astype(F32)).astype(BF)
        self.near = self.keep_near.astype(F32) + hop(self.send_near, "tok", 1, (), end).astype(F32)

    def along_x(self, begin=(), end=()):
        near = self.near + hop(self.away, "dp", 1, begin, end).astype(F32)
        self.low = jnp.stack([near[1], near[3]]).astype(BF)
        self.near = jnp.stack([near[0], near[2]])

    def near_z(self, begin=(), end=()):
        near = self.near + hop(self.low, "dp", 2, begin, end).astype(F32)
        self.low = near[1].astype(BF)
        self.near = near[0]

    def far_z(self, begin=(), end=()):
        self.mine = (self.near + hop(self.low, "dp", 4, begin, end).astype(F32)).astype(BF)

    def along_y(self, begin=(), end=()):
        other = hop(self.mine, "tok", 2, begin, end)
        self.mine = (self.mine.astype(F32) + other.astype(F32)).astype(BF)

    def halves(self, begin=(), end=()):
        return self.mine, hop(self.mine, "tok", 1, begin, end)


def adamw(weight, moments, clipped, rate, decay):
    first_mom = 0.9 * moments[0] + 0.1 * clipped
    second_mom = 0.999 * moments[1] + 0.001 * clipped * clipped
    fixed_first = first_mom / (1.0 - 0.9**STEP)
    fixed_second = second_mom / (1.0 - 0.999**STEP)
    new_weight = weight - rate * (fixed_first / (jnp.sqrt(fixed_second) + 1e-08) + decay * weight)
    return (jnp.stack([new_weight, first_mom]), second_mom)


FLAT = 128


def flatten_rows(ref, n, wide, out, base):
    period = math.lcm(wide, FLAT) // wide
    lines = period * wide // FLAT
    lane = lax.broadcasted_iota(jnp.int32, (n // period, FLAT), 1)
    for r in range(lines):
        value = jnp.zeros((n // period, FLAT), F32)
        for j in range(period):
            low, high = max(FLAT * r, wide * j), min(FLAT * (r + 1), wide * (j + 1))
            while low < high:
                column, at = low - wide * j, low - FLAT * r
                stop = min(high, low + FLAT - column % FLAT)
                part = ref[column // FLAT, pl.ds(j, n // period, stride=period), :]
                shift = (at - column) % FLAT
                part = pltpu.roll(part, shift, 1) if shift else part
                value = jnp.where(jnp.logical_and(lane >= at, lane < at + stop - low), part, value)
                low = stop
        out[pl.ds(base + r, n // period, stride=lines), :] = value
    return base + n * wide // FLAT


def tail_rows(pos, att, mlp, more):
    size = att[0].shape[0] - (0 if more is None else 8)

    def body(pos, att_mine, att_other, mlp_mine, mlp_other, *refs):
        out = refs[-1]
        total = jnp.zeros((1, D), F32)
        for ref in (att_mine, att_other, mlp_mine, mlp_other):
            rows = size if ref.shape[0] == size + 8 else ref.shape[0]
            value = ref[0:rows, :].astype(F32)
            total = total + jnp.sum(value * value, 0, keepdims=True)
        out[...] = jnp.zeros_like(out)
        if more is None:
            out[4:5, :] = total
        else:
            out[4:5, :] = total + refs[0][4:5, :]
            first = pos[2] == 0
            mine, other = att_mine[size : size + 8, :].astype(F32), att_other[size : size + 8, :].astype(F32)
            out[0:2, :] = jnp.where(first, mine, other)[0:2, :]
            out[2:4, :] = jnp.where(first, other, mine)[0:2, :]

    extra = () if more is None else (more,)
    return call(body, "tail_rows", [anywhere((8, D), F32)], [], 1, pos, *att, *mlp, *extra)[0]


def place_lanes(target, value, at):
    n = target.shape[1]
    value = jnp.concatenate([value, jnp.zeros((1, n - value.shape[1]), F32)], 1)
    lane = lax.broadcasted_iota(jnp.int32, (1, n), 1)
    return jnp.where(lane >= at, pltpu.roll(value, at, 1) if at else value, target)


def apply_adamw(pos, near, far, grads, masters, moments):
    big, small = range(4), (4, 5)
    out_shapes = [m.shape for m in moments]
    lines = [math.prod(t.shape) // FLAT for t in masters[:4]]
    gain_cols, bias_cols = masters[4].shape[-1], masters[5].shape[-1]
    small_size = LAYERS * (2 * gain_cols + bias_cols)
    total_lines = sum(lines) + small_size // FLAT
    att_rows = masters[0].shape[1] + masters[1].shape[1]

    def update(w, first, second, c, rate, decay):
        first = 0.9 * first + 0.1 * c
        second = 0.999 * second + 0.001 * c * c
        root = jnp.sqrt(second * (1.0 / (1.0 - 0.999**STEP))) + 1e-08
        return w - rate * (first * (1.0 / (1.0 - 0.9**STEP)) / root + decay * w), first, second

    def body(pos, near, far, *refs):
        g_refs = (refs[0:4], refs[4:8])
        gains_w, biases_w, gains_m, biases_m = refs[8:12]
        w_hbm, m_hbm = refs[12:16], refs[16:20]
        norm_out, gains_out, biases_out = refs[20:23]
        s_hbm, second_hbm = refs[23:27], refs[27]
        w_vm, m_vm, s_vm = refs[28:32], refs[32:36], refs[36:40]
        second_vm, whole, padded, in_sem, out_sem = refs[40:45]
        loads = [
            (pltpu.make_async_copy(w_hbm[i], w_vm[i], in_sem.at[0, i]), pltpu.make_async_copy(m_hbm[i], m_vm[i], in_sem.at[1, i]))
            for i in big
        ]
        for pair in loads:
            for copy in pair:
                copy.start()
        total = jnp.zeros((1, D), F32)
        for shard in range(8):
            z_rel = pos[0] ^ (shard // 2)
            rows = jnp.where(pos[1] == shard % 2, near[z_rel], far[z_rel])
            for layer in range(LAYERS):
                whole[layer, 2 * shard : 2 * shard + 2, :] = rows[2 * layer : 2 * layer + 2, :]
            total = total + rows[4:5, :]
        for layer in range(LAYERS):
            total = total + jnp.sum(whole[layer] * whole[layer], 0, keepdims=True)
        norm = jnp.sqrt(jnp.sum(total, 1, keepdims=True))
        norm_out[...] = jnp.broadcast_to(norm, norm_out.shape)
        factor = clip_factor(norm)
        stores, base = [], 0
        for i in big:
            for copy in loads[i]:
                copy.wait()
            n = masters[i].shape[1]
            for layer in range(LAYERS):
                att_mine, att_other, mlp_mine, mlp_other = g_refs[layer]
                zero = pos[2] == 0
                if i < 2:
                    size = att_rows // 2
                    low = jnp.where(zero, att_mine[0:size, :], att_other[0:size, :])
                    high = jnp.where(zero, att_other[0:size, :], att_mine[0:size, :])
                    g = jnp.concatenate([low, high], 0)
                    g = g[0:n] if i == 0 else g[att_rows - n :]
                else:
                    g = jnp.where(zero, (mlp_mine, mlp_other)[i - 2][...], (mlp_other, mlp_mine)[i - 2][...])
                new = update(w_vm[i][layer], m_vm[i][0, layer], m_vm[i][1, layer], g.astype(F32) * factor, 0.08, 0.05)
                s_vm[i][0, layer], s_vm[i][1, layer] = new[0], new[1]
                second = new[2] if i == 3 else new[2].T
                rows, cols = second.shape
                for at in range(0, cols, FLAT):
                    stop = min(at + FLAT, cols)
                    padded[at // FLAT, 0:rows, 0 : stop - at] = second[:, at:stop]
                base = flatten_rows(padded, rows, cols, second_vm, base)
            stores.append(pltpu.make_async_copy(s_vm[i], s_hbm[i], out_sem.at[i]))
            stores[-1].start()
        shard = pos[0] * 2 + pos[1]
        first_row = shard * 10 // 8
        flat = jnp.zeros((1, small_size), F32)
        for layer in range(LAYERS):
            rows = whole[layer]
            index = lax.broadcasted_iota(jnp.int32, rows.shape, 0)
            both = [jnp.sum(jnp.where(index == first_row + k, rows, 0.0), 0, keepdims=True) for k in range(2)]
            both = jnp.concatenate(both, 1)
            bias = both
            for k in range(1, 4):
                bias = jnp.where(shard % 4 == k, pltpu.roll(both, 2 * D - k * (D // 4), 1), bias)
            new = update(
                biases_w[layer : layer + 1, :], biases_m[0, layer : layer + 1, :], biases_m[1, layer : layer + 1, :],
                bias[:, 0:bias_cols] * factor, 0.4, 0.0,
            )
            biases_out[0, layer : layer + 1, :], biases_out[1, layer : layer + 1, :] = new[0], new[1]
            flat = place_lanes(flat, new[2], 2 * LAYERS * gain_cols + layer * bias_cols)
        seconds = []
        for layer in range(LAYERS):
            for which in range(2):
                row = whole[layer, GAIN1 + which : GAIN1 + which + 1, :]
                gain = row
                for k in range(1, 8):
                    gain = jnp.where(shard == k, pltpu.roll(row, D - k * gain_cols, 1), gain)
                new = update(
                    gains_w[layer, which : which + 1, :], gains_m[0, layer, which : which + 1, :],
                    gains_m[1, layer, which : which + 1, :], gain[:, 0:gain_cols] * factor, 0.4, 0.0,
                )
                gains_out[0, layer, which : which + 1, :], gains_out[1, layer, which : which + 1, :] = new[0], new[1]
                seconds.append(new[2])
        lane = lax.broadcasted_iota(jnp.int32, flat.shape, 1)
        head = jnp.concatenate(seconds + [jnp.zeros((1, small_size - len(seconds) * gain_cols), F32)], 1)
        flat = jnp.where(lane < len(seconds) * gain_cols, head, flat)
        for r in range(small_size // FLAT):
            second_vm[base + r : base + r + 1, :] = flat[:, r * FLAT : (r + 1) * FLAT]
        last = pltpu.make_async_copy(second_vm, second_hbm, out_sem.at[4])
        last.start()
        for copy in stores + [last]:
            copy.wait()

    flat_grads = [t for layer in grads for pair in layer for t in pair]
    smem, vmem, hbm = (pl.BlockSpec(memory_space=m) for m in (pltpu.SMEM, pltpu.VMEM, pl.ANY))
    return pl.pallas_call(
        body,
        name="apply_adamw",
        out_shape=[anywhere((8, FLAT), F32)] + [anywhere(out_shapes[i], F32) for i in small]
        + [anywhere(out_shapes[i], F32) for i in big] + [anywhere((total_lines, FLAT), F32)],
        in_specs=[smem] + [vmem] * (2 + len(flat_grads) + 4) + [hbm] * 8,
        out_specs=[vmem] * 3 + [hbm] * 5,
        scratch_shapes=[on_chip(masters[i].shape, F32) for i in big] + [on_chip(out_shapes[i], F32) for i in big] * 2
        + [on_chip((total_lines, FLAT), F32), on_chip((LAYERS, SMALL, D), F32), on_chip((D // FLAT, D, FLAT), F32),
           pltpu.SemaphoreType.DMA((2, 4)), pltpu.SemaphoreType.DMA((5,))],
        compiler_params=pltpu.CompilerParams(vmem_limit_bytes=24 << 20),
    )(pos, near, far, *flat_grads, *masters[4:], *moments[4:], *masters[:4], *moments[:4])


def clip_factor(norm):
    limit = 0.25 * math.sqrt(LAYERS * (4 * D * D + 2 * D * FF + 8 * D + FF))
    return jnp.minimum(1.0, limit / (norm + 1e-06))


def whole_small(gains, biases):
    rows = jnp.concatenate([biases.reshape(10, D), gains]).astype(F32)
    return jnp.pad(rows, ((0, SMALL - 12), (0, 0)))


def on_device(x, cot, lengths, w_qkv, w_proj, w_fc1, w_fc2, norm_gains, biases,
              mom_qkv, mom_proj, mom_fc1, mom_fc2, mom_gains, mom_biases):
    fast = fast_mesh()
    seqs, slots = x.shape[0], x.shape[1]
    own = lax.dynamic_slice_in_dim(lengths, lax.axis_index("tok") * seqs, seqs, 0)
    k = Kernels(plan_rows(own), seqs, slots)
    dp_index = lax.axis_index("dp")
    if fast:
        place = Place()
        att_parts, mlp_parts = Parts("att", place.pos), Parts("mlp", place.pos)

        def half(rows):
            size = rows.shape[0] // 2
            return lax.dynamic_slice_in_dim(rows, place.core * size, size, 0)

        small = spread_small(norm_gains, biases, dp_index)
        att = [half(jnp.concatenate([w_qkv[l].T, w_proj[l].T])) for l in range(LAYERS)]
        mlp = [jnp.where(place.core == 0, w_fc1[l].T, w_fc2[l]) for l in range(LAYERS)]
        size = att[0].shape[0]
        ga0 = Gather(jnp.concatenate([att[0], small]).astype(BF))
        gm0, ga1, gm1 = Gather(mlp[0].astype(BF)), Gather(att[1].astype(BF)), Gather(mlp[1].astype(BF))
        ga0.along_z()
        gm0.far_z((ga0.near,), (ga0.near,))
        ga0.along_x()
        gm0.near_z((ga0.far,))
        ga1.far_z((ga0.far,), (ga0.far,))
        att_w0, vec0, vec1 = assemble("att", place.pos, ga0.cores(), True)
    else:
        att_parts = mlp_parts = None

        def whole(w, axis):
            return lax.all_gather(w.astype(BF), "dp", axis=axis, tiled=True)

        full = [whole(w, 2) for w in (w_qkv, w_proj, w_fc1)] + [whole(w_fc2, 1)]
        gains_all, biases_all = whole(norm_gains, 2), whole(biases, 1)
        att_w0, att_w1 = (jnp.concatenate([full[0][l].T, full[1][l].T]) for l in range(LAYERS))
        mlp_w0, mlp_w1 = (jnp.concatenate([full[2][l].T, full[3][l]]) for l in range(LAYERS))
        vec0, vec1 = (whole_small(gains_all[l], biases_all[l]) for l in range(LAYERS))

    h0, a0, qkv0 = k.qkv_first(x, vec0, att_w0)
    if fast:
        gm0.near = after(gm0.near, qkv0)
        gm0.along_x((), ())
        ga1.near_z((qkv0,), ())
        gm1.far_z((qkv0,), ())
    o0, lse0 = k.attend(qkv0)
    if fast:
        gm0.far, ga1.near, gm1.pair = after(gm0.far, o0), after(ga1.near, o0), after(gm1.pair, o0)
        mlp_w0, = assemble("mlp", place.pos, gm0.cores(), False)
        ga1.along_x((mlp_w0,), ())
        gm1.near_z((mlp_w0,), ())
    mid0, b0, act0, slope0, h1 = k.mlp(h0, o0, vec0, att_w0, mlp_w0)
    cot_rows = k.pack(cot)
    if fast:
        ga1.far, gm1.near = after(ga1.far, h1), after(gm1.near, h1)
        att_w1, = assemble("att", place.pos, ga1.cores(), False)
        gm1.along_x((att_w1,), ())
    a1, qkv1, o1, lse1 = k.qkv_attend(h1, vec1, att_w1)
    if fast:
        gm1.far = after(gm1.far, o1)
        mlp_w1, = assemble("mlp", place.pos, gm1.cores(), False)
    mid1, b1, act1, slope1, h2 = k.mlp(h1, o1, vec1, att_w1, mlp_w1)
    (g1, dp, do, small1a), mlp1 = k.mlp_back(
        "mlp_back1", cot_rows, mid1, slope1, vec1, att_w1, mlp_w1, b1, act1, mlp_parts
    )
    if fast:
        sm1 = Scatter(mlp1)
        sm1.cores()
        k.wait(sm1.away)
    (g, small1b), att1 = k.attention_back(
        "attention_back1", qkv1, do, lse1, h1, g1, vec1, att_w1, a1, dp, o1, att_parts
    )
    if fast:
        sm1.along_x((), (g,))
        sa1 = Scatter(att1)
        sa1.cores()
        k.wait(sa1.away, sm1.low)
    (g1, dp, do, small0a), mlp0 = k.mlp_back(
        "mlp_back0", g, mid0, slope0, vec0, att_w0, mlp_w0, b0, act0, mlp_parts
    )
    if fast:
        sm1.near_z((), (g1,))
        sa1.along_x((sm1.near,), (g1,))
        sm0 = Scatter(mlp0)
        sm0.cores()
        k.wait(sm0.away, sm1.low, sa1.low)
    smalls = (small0a, small1a, small1b) if fast else ()
    (g, small0b), att0 = k.attention_back(
        "attention_back0", qkv0, do, lse0, h0, g1, vec0, att_w0, a0, dp, o0, att_parts, smalls
    )
    if fast:
        sm0.along_x((), (g,))
        sm1.far_z((), (g,))
        sa1.near_z((), (g,))
        k.wait(sm0.low, sm1.mine, sa1.low, att0)
    input_grad = k.unpack("unpack_grad", g, F32)
    layer_out = k.unpack("unpack_out", h2, BF)

    if fast:
        sa0 = Scatter(att0)
        sa0.cores()
        sa0.along_x((sm0.low,), (input_grad, layer_out))
        sm0.near_z((sa0.away,), (input_grad, layer_out))
        sa1.far_z((sa0.away,), (input_grad, layer_out))
        sm1.along_y((sa0.away,), (input_grad, layer_out))
        sa0.near_z((sm0.low,))
        sm0.far_z((sa0.low,))
        sa1.along_y((sa0.low,))
        h_mlp1 = sm1.halves((sa0.low,))
        sa0.far_z((sm0.mine,))
        sm0.along_y((sm0.mine,))
        h_att1 = sa1.halves((sm0.mine,))
        sa0.along_y((sm0.mine,))
        h_mlp0 = sm0.halves((sa0.mine,))
        part = tail_rows(place.pos, h_att1, h_mlp1, None)
        h_att0 = sa0.halves()
        tail = Gather(tail_rows(place.pos, h_att0, h_mlp0, part))
        tail.along_z()
        tail_far = swap(tail.near, "dp", 1)
    else:
        small_g = lax.psum(jnp.stack([small0a + small0b, small1a + small1b]), ("dp", "tok"))

        def part(rows):
            return lax.psum(lax.psum_scatter(rows.astype(F32), "dp", scatter_dimension=0, tiled=True), "tok")

        grads = [
            jnp.stack([part(t[: 3 * D]).T for (t,) in (att0, att1)]),
            jnp.stack([part(t[3 * D :]).T for (t,) in (att0, att1)]),
            jnp.stack([part(t[:FF]).T for (t,) in (mlp0, mlp1)]),
            jnp.stack([part(t[FF:]) for (t,) in (mlp0, mlp1)]),
        ]
        squares = lax.psum(sum(jnp.sum(t * t) for t in grads), "dp") + jnp.sum(small_g * small_g)
    masters = (w_qkv, w_proj, w_fc1, w_fc2, norm_gains, biases)
    moments = (mom_qkv, mom_proj, mom_fc1, mom_fc2, mom_gains, mom_biases)
    if fast:
        turned = [w.swapaxes(-1, -2) if i < 3 else w for i, w in enumerate(masters)]
        turned_moments = [m.swapaxes(-1, -2) if i < 3 else m for i, m in enumerate(moments)]
        halves = ((h_att0, h_mlp0), (h_att1, h_mlp1))
        norm, gains, rows, *states, seconds = apply_adamw(
            place.pos, tail.near, tail_far, halves, turned, turned_moments
        )
        states = [t.swapaxes(-1, -2) if i < 3 else t for i, t in enumerate(states)] + [gains, rows]
        return (layer_out, input_grad, norm[0, 0], *states, seconds.reshape(-1))
    gains_g = small_g[:, GAIN1 : GAIN2 + 1]
    biases_g = small_g[:, :10].reshape(LAYERS, -1)
    grads.append(lax.dynamic_slice_in_dim(gains_g, dp_index * norm_gains.shape[2], norm_gains.shape[2], 2))
    grads.append(lax.dynamic_slice_in_dim(biases_g, dp_index * biases.shape[1], biases.shape[1], 1))
    grad_norm = jnp.sqrt(squares)
    factor = clip_factor(grad_norm)
    pairs = [
        adamw(w, m, t * factor, 0.08 if i < 4 else 0.4, 0.05 if i < 4 else 0.0)
        for i, (w, m, t) in enumerate(zip(masters, moments, grads))
    ]
    seconds = jnp.concatenate([second.reshape(-1) for _, second in pairs])
    return (layer_out, input_grad, grad_norm, *(state for state, _ in pairs), seconds)


def solution(mesh):
    rows = P(("dp", "tok"), None, None)
    weights = (P(None, None, "dp"),) * 3 + (P(None, "dp", None), P(None, None, "dp"), P(None, "dp"))
    stacked = tuple(P(None, *spec) for spec in weights)
    return jax.shard_map(
        on_device,
        mesh=mesh,
        in_specs=(rows, rows, P("dp"), *weights, *stacked),
        out_specs=(rows, rows, P(), *stacked, P("dp")),
        check_vma=False,
    )
```
